32 devices in a mesh: dp: 32 (over z, y, x, core).
Axes of the slice: x: 2, y: 2, z: 4, core: 2. Of those that a mesh axis runs over, the one named last changes fastest.
Arguments:
- params: float32 [1774080], P('dp')
- images: bfloat16 [256, 197, 384], P('dp'), may hold values from -6 to 6
- cotangent: bfloat16 [256, 197, 384], P('dp'), may hold values from -6 to 6
- live: int32 [32], P('dp'), may hold values from 1 to 8, as said below
Outputs:
- layer_out: bfloat16 [256, 197, 384], P('dp')
- input_grad: bfloat16 [256, 197, 384], P('dp')
- flat_parameter_gradient: float32 [1774080], P('dp')
The draws below stay inside these ranges and needn't reach their ends.
Inputs may be any that keep to these rules, and one draw needn't show every extreme that they name: The first live[d] of device d's 8 slots hold images; every draw has a device with all 8 slots occupied.
All inputs are finite; a program needn't handle non-finite values.
Results may differ from the reference program's by a relative error of at most 0.0098.
Values may be sent and summed in bfloat16 or wider, within the bound.
A program may use at most 192 MiB of HBM per device.

```python
import jax
import jax.numpy as jnp
from jax import lax

D = 384
HEADS = 6
FF = 1536
TOK = 197
IMG_DEV = 8
SLOTS = 256
PARAMS = 1774080
N_DP = 32


def draw_params(key, part):
    subkeys = jax.random.split(key, 16)

    def rough_draw(number, count, scale):
        return jax.random.normal(subkeys[number], (count,), jnp.float32) * scale

    def gain_draw(number):
        return 1.0 + 0.4 * jax.random.uniform(subkeys[number], (D,), jnp.float32, -1.0, 1.0)
    w_qkv = rough_draw(2, D * 3 * D, D ** (-0.5)).reshape(D, 3 * D)
    pieces = [gain_draw(0), rough_draw(1, D, 0.3), w_qkv.reshape(-1), rough_draw(3, D, 0.3), rough_draw(4, D, 0.3), rough_draw(5, D * D, 3.0 * D ** (-0.5)), rough_draw(6, D, 0.3), gain_draw(7), rough_draw(8, D, 0.3), rough_draw(9, D * FF, D ** (-0.5)), rough_draw(10, FF, 0.3), rough_draw(11, FF * D, FF ** (-0.5)), rough_draw(12, D, 0.3)]
    used = 4 * D * D + 2 * D * FF + 8 * D + FF
    pieces.append(rough_draw(13, PARAMS - used, 1.0))
    return jnp.concatenate(pieces)


def draw_live(key, part):
    devices = SLOTS // IMG_DEV
    counts = jax.random.randint(jax.random.fold_in(key, 1), (devices,), 1, IMG_DEV + 1)
    chosen = jax.random.randint(jax.random.fold_in(key, 2), (), 0, devices)
    return counts.at[chosen].set(IMG_DEV).astype(jnp.int32)


def steps_of(key, shape, cuts, low, high):
    loudness = 1.0
    for dim, parts in cuts:
        heights = jax.random.uniform(jax.random.fold_in(jax.random.fold_in(key, 6), dim), (parts,), jnp.float32, low / len(cuts), high / len(cuts))
        loudness = loudness * jnp.repeat(jnp.exp(heights), shape[dim] // parts).reshape((-1,) + (1,) * (len(shape) - 1 - dim))
    return loudness


def gaussian(key, shape, scale, most, shards=(), kind=jnp.bfloat16):
    entries = jax.random.normal(key, shape, jnp.float32) * scale
    if len(shards) > 0:
        entries = steps_of(key, shape, shards, -0.22, 0.18) * entries
    return jnp.clip(entries, min=-most, max=most).astype(kind)


def setup_inputs(seed: int = 0) -> dict:
    arg_keys = jax.random.split(jax.random.key(seed), 5)
    return {
        "params": draw_params(jax.random.fold_in(arg_keys[4], 71), 0),
        "images": gaussian(arg_keys[1], (SLOTS, TOK, D), 1.0, 6.0, ((0, 32),)),
        "cotangent": gaussian(arg_keys[2], (SLOTS, TOK, D), 1.0, 6.0, ((0, 32),)),
        "live": draw_live(jax.random.fold_in(arg_keys[4], 71), 0),
    }


EPS = 1e-06

def norm_rows(values, gain, shift):
    center = values - lax.optimization_barrier(jnp.mean(values, axis=-1, keepdims=True))
    inv_std = lax.rsqrt(lax.optimization_barrier(jnp.mean(center * center, axis=-1, keepdims=True)) + EPS)
    normed = center * inv_std
    return (normed * gain + shift, normed, inv_std)

def norm_back(grad_out, normed, inv_std, gain):
    grad_hat = grad_out * gain
    return inv_std * (grad_hat - lax.optimization_barrier(jnp.mean(grad_hat, axis=-1, keepdims=True)) - normed * lax.optimization_barrier(jnp.mean(grad_hat * normed, axis=-1, keepdims=True)))

def unpack(weights):
    widths = [D, D, D * 3 * D, D, D, D * D, D, D, D, D * FF, FF, FF * D, D]
    pieces = []
    start = 0
    for width in widths:
        pieces.append(weights[start:start + width])
        start = start + width
    pieces[2] = pieces[2].reshape(D, 3 * D)
    pieces[5] = pieces[5].reshape(D, D)
    pieces[9] = pieces[9].reshape(D, FF)
    pieces[11] = pieces[11].reshape(FF, D)
    return pieces

def forward_sweep(weights, images):
    gain_one, shift_one, w_qkv, bias_q, bias_v, w_out, bias_out, gain_two, shift_two, w_up, bias_up, w_down, bias_down = unpack(weights)
    batch, length = (images.shape[0], images.shape[1])
    head_dim = D // HEADS
    inputs = images.astype(jnp.float32)
    normed_one, hat_one, inv_one = norm_rows(inputs, gain_one, shift_one)
    attn_in = normed_one.astype(jnp.bfloat16)
    bias_all = jnp.concatenate([bias_q, jnp.zeros_like(bias_q), bias_v]).astype(jnp.float32)
    project = jnp.einsum('btd,de->bte', attn_in, w_qkv, preferred_element_type=jnp.float32) + bias_all
    batched_projection = project.astype(jnp.bfloat16)
    query = batched_projection[..., :D].reshape(batch, length, HEADS, head_dim)
    keys_all = batched_projection[..., D:2 * D].reshape(batch, length, HEADS, head_dim)
    values_all = batched_projection[..., 2 * D:].reshape(batch, length, HEADS, head_dim)
    scale = head_dim ** (-0.5)
    scores = jnp.einsum('bqhd,bkhd->bhqk', query, keys_all, preferred_element_type=jnp.float32) * scale
    log_total = jax.nn.logsumexp(scores, axis=-1)
    probs_b = jnp.exp(scores - log_total[..., None]).astype(jnp.bfloat16)
    mixed = jnp.einsum('bhqk,bkhd->bqhd', probs_b, values_all, preferred_element_type=jnp.float32)
    mixed_b = mixed.reshape(batch, length, D).astype(jnp.bfloat16)
    hidden = inputs + jnp.einsum('btd,de->bte', mixed_b, w_out, preferred_element_type=jnp.float32) + bias_out.astype(jnp.float32)
    normed_two, hat_two, inverse_std_second = norm_rows(hidden, gain_two, shift_two)
    ffn_in = normed_two.astype(jnp.bfloat16)
    pre_act = jnp.einsum('btd,df->btf', ffn_in, w_up, preferred_element_type=jnp.float32) + bias_up.astype(jnp.float32)
    act_b = jax.nn.gelu(pre_act, approximate=False).astype(jnp.bfloat16)
    result = hidden + jnp.einsum('btf,fd->btd', act_b, w_down, preferred_element_type=jnp.float32) + bias_down.astype(jnp.float32)
    saved_activation = (hat_one, inv_one, attn_in, batched_projection, log_total, mixed_b, hat_two, inverse_std_second, ffn_in, pre_act, act_b)
    return (result, saved_activation)

def reverse_sweep(weights, saved_activation, cotangent, mask):
    gain_one, shift_one, w_qkv, bias_q, bias_v, w_out, bias_out, gain_two, shift_two, w_up, bias_up, w_down, bias_down = unpack(weights)
    hat_one, inv_one, attn_in, batched_projection, log_total, mixed_b, hat_two, inverse_std_second, ffn_in, pre_act, act_b = saved_activation
    batch, length = (cotangent.shape[0], cotangent.shape[1])
    head_dim = D // HEADS
    scale = head_dim ** (-0.5)
    dout = cotangent.astype(jnp.float32) * mask[:, None, None]
    dout_b = dout.astype(jnp.bfloat16)
    grad_down = jnp.einsum('btf,btd->fd', act_b, dout_b, preferred_element_type=jnp.float32)
    grad_bias_down = lax.optimization_barrier(jnp.sum(dout, axis=(0, 1)))
    dact = jnp.einsum('btd,fd->btf', dout_b, w_down, preferred_element_type=jnp.float32)
    cumul = 0.5 * (1.0 + lax.erf(pre_act * 0.7071067811865476))
    density = jnp.exp(-0.5 * pre_act * pre_act) * 0.3989422804014327
    dpre = dact * (cumul + pre_act * density)
    dpre_b = dpre.astype(jnp.bfloat16)
    grad_up = jnp.einsum('btd,btf->df', ffn_in, dpre_b, preferred_element_type=jnp.float32)
    grad_bias_up = lax.optimization_barrier(jnp.sum(dpre, axis=(0, 1)))
    dnorm_two = jnp.einsum('btf,df->btd', dpre_b, w_up, preferred_element_type=jnp.float32)
    grad_gain_two = lax.optimization_barrier(jnp.sum(dnorm_two * hat_two, axis=(0, 1)))
    grad_shift_two = lax.optimization_barrier(jnp.sum(dnorm_two, axis=(0, 1)))
    dhidden = dout + norm_back(dnorm_two, hat_two, inverse_std_second, gain_two)
    dhidden_b = dhidden.astype(jnp.bfloat16)
    grad_out = jnp.einsum('btd,bte->de', mixed_b, dhidden_b, preferred_element_type=jnp.float32)
    grad_bias_out = lax.optimization_barrier(jnp.sum(dhidden, axis=(0, 1)))
    dmixed = jnp.einsum('bte,de->btd', dhidden_b, w_out, preferred_element_type=jnp.float32)
    dmixed_b = dmixed.astype(jnp.bfloat16).reshape(batch, length, HEADS, head_dim)
    query = batched_projection[..., :D].reshape(batch, length, HEADS, head_dim)
    keys_all = batched_projection[..., D:2 * D].reshape(batch, length, HEADS, head_dim)
    values_all = batched_projection[..., 2 * D:].reshape(batch, length, HEADS, head_dim)
    scores = jnp.einsum('bqhd,bkhd->bhqk', query, keys_all, preferred_element_type=jnp.float32) * scale
    probs = jnp.exp(scores - log_total[..., None])
    probs_b = probs.astype(jnp.bfloat16)
    dvalue = jnp.einsum('bhqk,bqhd->bkhd', probs_b, dmixed_b, preferred_element_type=jnp.float32)
    dprobs = jnp.einsum('bqhd,bkhd->bhqk', dmixed_b, values_all, preferred_element_type=jnp.float32)
    delta = lax.optimization_barrier(jnp.sum(probs * dprobs, axis=-1, keepdims=True))
    dscores_b = (probs * (dprobs - delta) * scale).astype(jnp.bfloat16)
    dquery = jnp.einsum('bhqk,bkhd->bqhd', dscores_b, keys_all, preferred_element_type=jnp.float32)
    dkey = jnp.einsum('bhqk,bqhd->bkhd', dscores_b, query, preferred_element_type=jnp.float32)
    dqkv = jnp.concatenate([dquery.reshape(batch, length, D), dkey.reshape(batch, length, D), dvalue.reshape(batch, length, D)], axis=-1)
    dqkv_b = dqkv.astype(jnp.bfloat16)
    grad_qkv = jnp.einsum('btd,bte->de', attn_in, dqkv_b, preferred_element_type=jnp.float32)
    grad_bias_q = lax.optimization_barrier(jnp.sum(dqkv[..., :D], axis=(0, 1)))
    grad_bias_v = lax.optimization_barrier(jnp.sum(dqkv[..., 2 * D:], axis=(0, 1)))
    dnorm_one = jnp.einsum('bte,de->btd', dqkv_b, w_qkv, preferred_element_type=jnp.float32)
    grad_gain_one = lax.optimization_barrier(jnp.sum(dnorm_one * hat_one, axis=(0, 1)))
    grad_shift_one = lax.optimization_barrier(jnp.sum(dnorm_one, axis=(0, 1)))
    dinput = dhidden + norm_back(dnorm_one, hat_one, inv_one, gain_one)
    pieces = [grad_gain_one, grad_shift_one, grad_qkv, grad_bias_q, grad_bias_v, grad_out, grad_bias_out, grad_gain_two, grad_shift_two, grad_up, grad_bias_up, grad_down, grad_bias_down]
    flat = jnp.concatenate([piece.reshape(-1) for piece in pieces])
    padding = jnp.zeros((weights.shape[0] - flat.shape[0],), jnp.float32)
    return (dinput.astype(jnp.bfloat16), jnp.concatenate([flat, padding]))

def reference(params, images, cotangent, live):
    weights = params.astype(jnp.bfloat16)
    masks = (jnp.arange(IMG_DEV, dtype=jnp.int32)[None, :] < live[:, None]).astype(jnp.float32)
    image_blocks = images.reshape(N_DP, IMG_DEV, TOK, D)
    cot_blocks = cotangent.reshape(N_DP, IMG_DEV, TOK, D)

    def step_block(total, block):
        image_block, cot_block, mask_block = block
        result, saved_activation = forward_sweep(weights, image_block)
        output = (result * mask_block[:, None, None]).astype(jnp.bfloat16)
        dinput, grads = reverse_sweep(weights, saved_activation, cot_block, mask_block)
        return (total + grads, (output, dinput))
    start = jnp.zeros((params.shape[0],), jnp.float32)
    total, (outputs, dinputs) = lax.scan(step_block, start, (image_blocks, cot_blocks, masks))
    return (outputs.reshape(SLOTS, TOK, D), dinputs.reshape(SLOTS, TOK, D), total)
```

```python
import functools

import jax
import jax.numpy as jnp
from jax import lax
from jax.experimental import pallas as pl
from jax.experimental.pallas import tpu as pltpu
from jax.sharding import PartitionSpec as P

D = 384
HEADS = 6
FF = 1536
HD = D // HEADS
PAIRS = HEADS // 2
EPS = 1e-06
LANES = 128
BF = jnp.bfloat16
F32 = jnp.float32

ROW_QKV = 2
ROW_OUT = 2 + 3 * D + 2
ROW_UP = ROW_OUT + D + 3
ROW_BUP = ROW_UP + FF
ROW_DOWN = ROW_BUP + FF // D
ROW_BDOWN = ROW_DOWN + FF
ROWS = ROW_BDOWN + 1
VEC_ROWS = (0, 1, ROW_OUT - 2, ROW_OUT - 1, ROW_UP - 3, ROW_UP - 2, ROW_UP - 1, ROW_BDOWN)
G1, S1, BQ, BV, BO, G2, S2, BD = range(8)

CHUNK = 256
PARTS = 4
UNROLL = 2
BLOCKS = 4
MESH = pl.DeviceIdType.MESH


def up_to(value, unit):
    return (value + unit - 1) // unit * unit


def nt(a, b):
    return lax.dot_general(a, b, (((1,), (1,)), ((), ())), preferred_element_type=F32)


def tn(a, b):
    return lax.dot_general(a, b, (((0,), (0,)), ((), ())), preferred_element_type=F32)


def nn(a, b):
    return jnp.dot(a, b, preferred_element_type=F32)


def norm_stats(values):
    center = values - jnp.mean(values, axis=-1, keepdims=True)
    inv = lax.rsqrt(jnp.mean(center * center, axis=-1, keepdims=True) + EPS)
    return center * inv, inv


def norm_back(grad_out, hat, inv, gain):
    g = grad_out * gain
    return inv * (
        g
        - jnp.mean(g, axis=-1, keepdims=True)
        - hat * jnp.mean(g * hat, axis=-1, keepdims=True)
    )


def colsum(v):
    return jnp.sum(v, axis=0, keepdims=True)


def part_orders(bits):
    near = list(range(bits))
    swapped = near[:1] + near[2:3] + near[1:2] + near[3:]
    orders = [near, swapped]
    for order in (near, swapped):
        orders.append(order[:2] + order[3:4] + order[2:3] + order[4:])
    return orders


def matrices():
    return (
        (0, D, 9, ROW_QKV),
        (1, D, 3, ROW_OUT),
        (2, D, 12, ROW_UP),
        (3, FF, 3, ROW_DOWN),
    )


def step_kernel(
    n, shard, slots, tok, tokp,
    live_ref, mine_ref, img_hbm, cot_hbm,
    out_ref, din_ref, flat_ref,
    gath, recv, buf, wqkv, wout, wup, wdn, vec, bup, gvec,
    img_v, cot_v, stage, x_s, dout_s, attn_s, qkv_s, probs_s, mixed_s,
    hat_s, inv_s, res_s, dn2_s, ffn_s,
    load_sem, gsend, grecv, rsend, rrecv,
):
    bits = n.bit_length() - 1
    me = lax.axis_index("dp")
    window = mine_ref.shape[0]
    part = window // PARTS
    weights = (wqkv, wout, wup, wdn)
    early = -(-3 * ROW_OUT * LANES // shard)
    delta = [(1 - 2 * (me // (1 << b) % 2)) * (1 << b) for b in range(bits)]
    r_orders = part_orders(bits)
    g_orders = [order[::-1] for order in r_orders]

    def in_wave(block, wave):
        return block < early if wave == 0 else block >= early

    def spread(k, dims):
        return sum(((k // (1 << i)) % 2) * delta[b] for i, b in enumerate(dims))

    def each(count, body):
        if count == 1:
            body(0)
            return

        def step(k, carry):
            body(k)
            return carry

        lax.fori_loop(0, count, step, 0)

    def gather_copy(p, s, k, source, first):
        rows = pl.ds(p * part, part)
        slot = (1 << s) - 1 + k
        return pltpu.make_async_remote_copy(
            src_ref=mine_ref.at[rows] if first else gath.at[source, rows],
            dst_ref=gath.at[source, rows],
            send_sem=gsend.at[p, slot],
            recv_sem=grecv.at[p, slot],
            device_id=(me + delta[g_orders[p][s]],),
            device_id_type=MESH,
        )

    def gather_start(p, s, wave):
        def body(k):
            source = me + spread(k, g_orders[p][:s])

            @pl.when(in_wave(source, wave))
            def _():
                gather_copy(p, s, k, source, s == 0).start()

        each(1 << s, body)

    def gather_sent(p, s, wave):
        def body(k):
            source = me + spread(k, g_orders[p][:s])

            @pl.when(in_wave(source, wave))
            def _():
                gather_copy(p, s, k, source, s == 0).wait_send()

        each(1 << s, body)

    def gather_arrive(p, s, wave):
        def body(k):
            source = me + delta[g_orders[p][s]] + spread(k, g_orders[p][:s])

            @pl.when(in_wave(source, wave))
            def _():
                gather_copy(p, s, k, source, False).wait_recv()

        each(1 << s, body)

    def gather_round(s, wave):
        for p in range(PARTS):
            gather_arrive(p, s, wave)
            if s + 1 < bits:
                gather_start(p, s + 1, wave)

    def reduce_copy(p, s, k, block):
        slot = n - (n >> s) + k
        return pltpu.make_async_remote_copy(
            src_ref=gath.at[block, pl.ds(p * part, part)],
            dst_ref=recv.at[p, slot],
            send_sem=rsend.at[p, slot],
            recv_sem=rrecv.at[p, slot],
            device_id=(me + delta[r_orders[p][s]],),
            device_id_type=MESH,
        )

    def reduce_start(p, s, wave):
        order = r_orders[p]

        def body(k):
            block = me + delta[order[s]] + spread(k, order[s + 1 :])

            @pl.when(in_wave(block, wave))
            def _():
                reduce_copy(p, s, k, block).start()

        each(n >> (s + 1), body)

    def reduce_sent(p, s, wave):
        order = r_orders[p]

        def body(k):
            block = me + delta[order[s]] + spread(k, order[s + 1 :])

            @pl.when(in_wave(block, wave))
            def _():
                reduce_copy(p, s, k, block).wait_send()

        each(n >> (s + 1), body)

    def reduce_absorb(p, s, wave):
        rows = pl.ds(p * part, part)

        def body(k):
            block = me + spread(k, r_orders[p][s + 1 :])

            @pl.when(in_wave(block, wave))
            def _():
                reduce_copy(p, s, k, block).wait_recv()
                slot = n - (n >> s) + k
                total = gath[block, rows].astype(F32) + recv[p, slot].astype(F32)
                if s + 1 == bits:
                    flat_ref[rows, :] = total
                else:
                    gath[block, rows] = total.astype(BF)

        each(n >> (s + 1), body)

    def reduce_round(s, wave):
        for p in range(PARTS):
            reduce_absorb(p, s, wave)
            if s + 1 < bits:
                reduce_start(p, s + 1, wave)

    def unpack(blocks):
        for d in blocks:
            first, shift = divmod(shard * d, LANES)
            rows = (shift + shard + LANES - 1) // LANES
            piece = gath[d].astype(F32)
            if d > 0 and shift:
                seam = buf[first : first + 1, :] + piece[0:1]
                buf[first : first + rows, :] = piece[:rows]
                buf[first : first + 1, :] = seam
            else:
                buf[first : first + rows, :] = piece[:rows]

    def load_matrix(k, rows, blocks, start):
        for b in range(blocks):
            weights[k][:, b * LANES : (b + 1) * LANES] = buf[
                pl.ds(3 * start + b, rows, blocks), :
            ].astype(BF)

    def load_vectors(indices):
        for i in indices:
            r = VEC_ROWS[i]
            for c in range(3):
                vec[i : i + 1, c * LANES : (c + 1) * LANES] = buf[3 * r + c : 3 * r + c + 1, :]

    def put_vector(i, value):
        r = VEC_ROWS[i]
        for c in range(3):
            buf[3 * r + c : 3 * r + c + 1, :] = value[:, c * LANES : (c + 1) * LANES]

    def pack(blocks):
        for d in blocks:
            first = shard * d // LANES
            gath[d] = buf[first : first + window, :].astype(BF)

    def param(i):
        return vec[i : i + 1, :]

    loads = [
        pltpu.make_async_copy(img_hbm, img_v, load_sem.at[0]),
        pltpu.make_async_copy(cot_hbm, cot_v, load_sem.at[1]),
    ]
    for c in loads:
        c.start()
    barrier = pltpu.get_barrier_semaphore()
    for b in range(bits):
        pl.semaphore_signal(barrier, inc=1, device_id=(me + delta[b],), device_id_type=MESH)
    pl.semaphore_wait(barrier, bits)
    for wave in range(2):
        for p in range(PARTS):
            gather_start(p, 0, wave)
    gath[me] = mine_ref[...]

    def scatter_rows(source, target, scales):
        for c in range(3):
            stage[c] = source[:, c * LANES : (c + 1) * LANES].astype(F32)
        target[...] = jnp.zeros_like(target)
        for g in range(slots):
            for c in range(3):
                cols = slice(c * LANES, (c + 1) * LANES)
                v = stage[c, pl.ds(g, tok, slots), :]
                if scales is not None:
                    v = v * scales[g]
                target[g * tokp : g * tokp + tok, cols] = v.astype(BF)

    live = live_ref[0]
    masks = [(g < live).astype(F32) for g in range(slots)]
    loads[0].wait()
    scatter_rows(img_v, x_s, None)
    gather_round(0, 0)
    loads[1].wait()
    scatter_rows(cot_v, dout_s, masks)
    for s in range(1, bits):
        gather_round(s, 0)
    unpack(range(early))
    load_matrix(*matrices()[0])
    load_vectors((G1, S1, BQ, BV))
    gvec[...] = jnp.zeros_like(gvec)

    height = x_s.shape[0] // BLOCKS
    bias = jnp.concatenate([param(BQ), jnp.zeros((1, D), F32), param(BV)], axis=1)

    def band(i):
        return pl.ds(pl.multiple_of(i * height, 16), height)

    def project(i, carry):
        hat1, _ = norm_stats(x_s[band(i), :].astype(F32))
        attn_in = (hat1 * param(G1) + param(S1)).astype(BF)
        attn_s[band(i), :] = attn_in
        qkv_s[band(i), :] = (nn(attn_in, wqkv[...]) + bias).astype(BF)
        return carry

    lax.fori_loop(0, BLOCKS, project, 0)

    lane = lax.broadcasted_iota(jnp.int32, (1, LANES), 1)
    low = lane < HD
    low_b = low.astype(BF)
    high_b = 1 - low_b
    key_ok = lax.broadcasted_iota(jnp.int32, (1, tokp), 1) < tok

    def views(t):
        g, p = t // PAIRS, t % PAIRS
        rows = pl.ds(pl.multiple_of(g * tokp, 16), tokp)
        return rows, [pl.ds(pl.multiple_of(j * D + p * LANES, LANES), LANES) for j in range(3)]

    def stack(v, scale=1.0):
        return jnp.concatenate([v * (low_b * scale), v * (high_b * scale)], axis=0)

    def attend(t):
        rows, (cq, ck, cv) = views(t)
        q, k, v = qkv_s[rows, cq], qkv_s[rows, ck], qkv_s[rows, cv]
        s = nt(stack(q, HD**-0.5), k)
        s = jnp.where(key_ok, s, -1e30)
        e = jnp.exp(s - jnp.max(s, axis=-1, keepdims=True))
        probs = (e * (1.0 / jnp.sum(e, axis=-1, keepdims=True))).astype(BF)
        probs_s[t] = probs
        mixed = nn(probs, v)
        mixed_s[rows, cq] = jnp.where(low, mixed[:tokp], mixed[tokp:]).astype(BF)

    tiles = slots * PAIRS
    trips = tiles // UNROLL

    def forward(i, carry):
        for s in range(bits):
            @pl.when(i == (s * trips) // bits)
            def _():
                gather_round(s, 1)

        for u in range(UNROLL):
            attend(i * UNROLL + u)
        return carry

    lax.fori_loop(0, trips, forward, 0)
    for wave in range(2):
        for p in range(PARTS):
            for s in range(bits):
                gather_sent(p, s, wave)
    unpack(range(early, n))
    for m in matrices()[1:]:
        load_matrix(*m)
    load_vectors((BO, G2, S2, BD))
    for c in range(FF // LANES):
        bup[:, c * LANES : (c + 1) * LANES] = buf[3 * ROW_BUP + c : 3 * ROW_BUP + c + 1, :]
    tail = buf.shape[0] - 3 * ROWS
    buf[3 * ROWS :, :] = jnp.zeros((tail, LANES), F32)

    def add_vector(i, value):
        gvec[i : i + 1, :] += value

    def second_norm(i, carry):
        rows = band(i)
        hidden = x_s[rows, :].astype(F32) + nn(mixed_s[rows, :], wout[...]) + param(BO)
        hat2, inv2 = norm_stats(hidden)
        ffn_s[rows, :] = (hat2 * param(G2) + param(S2)).astype(BF)
        hat_s[rows, :] = hat2
        inv_s[rows, :] = inv2
        res_s[rows, :] = hidden + param(BD)
        dn2_s[rows, :] = jnp.zeros((height, D), F32)
        add_vector(BD, colsum(dout_s[rows, :].astype(F32)))
        return carry

    lax.fori_loop(0, BLOCKS, second_norm, 0)

    def feed(c, carry):
        cols = pl.ds(pl.multiple_of(c * CHUNK, CHUNK), CHUNK)
        ffn_in = ffn_s[...]
        dout_b = dout_s[...]
        pre = nn(ffn_in, wup[:, cols]) + bup[:, cols]
        cumul = 0.5 * (1.0 + lax.erf(pre * 0.7071067811865476))
        act = (pre * cumul).astype(BF)
        res_s[...] += nn(act, wdn[cols, :])
        grad = tn(act, dout_b)
        for b in range(3):
            buf[pl.ds(3 * ROW_DOWN + 3 * CHUNK * c + b, CHUNK, 3), :] = grad[
                :, b * LANES : (b + 1) * LANES
            ]
        density = jnp.exp(-0.5 * pre * pre) * 0.3989422804014327
        dpre = nt(dout_b, wdn[cols, :]) * (cumul + pre * density)
        total = colsum(dpre)
        dpre_b = dpre.astype(BF)
        grad = tn(ffn_in, dpre_b)
        for b in range(CHUNK // LANES):
            lanes = slice(b * LANES, (b + 1) * LANES)
            at = c * (CHUNK // LANES) + b
            buf[pl.ds(3 * ROW_UP + at, D, FF // LANES), :] = grad[:, lanes]
            buf[pl.ds(3 * ROW_BUP + at, 1), :] = total[:, lanes]
        dn2_s[...] += nt(dpre_b, wup[:, cols])
        return carry

    lax.fori_loop(0, FF // CHUNK, feed, 0)

    def gather_back(value, source_ref):
        for g in range(slots):
            for c in range(3):
                cols = slice(c * LANES, (c + 1) * LANES)
                v = source_ref[g * tokp : g * tokp + tok, cols]
                if value is not None:
                    v = v * value[g]
                stage[c, pl.ds(g, tok, slots), :] = v

    def emit_rows(target):
        for c in range(3):
            target[:, c * LANES : (c + 1) * LANES] = stage[c].astype(BF)

    def second_norm_back(i, carry):
        rows = band(i)
        hat2 = hat_s[rows, :]
        dn2 = dn2_s[rows, :]
        add_vector(G2, colsum(dn2 * hat2))
        add_vector(S2, colsum(dn2))
        dhidden = dout_s[rows, :].astype(F32) + norm_back(dn2, hat2, inv_s[rows, :], param(G2))
        dn2_s[rows, :] = dhidden
        dhidden_b = dhidden.astype(BF)
        add_vector(BO, colsum(dhidden))
        dout_s[rows, :] = dhidden_b
        ffn_s[rows, :] = nt(dhidden_b, wout[...]).astype(BF)
        return carry

    lax.fori_loop(0, BLOCKS, second_norm_back, 0)
    grad = tn(mixed_s[...], dout_s[...])
    for b in range(3):
        buf[pl.ds(3 * ROW_OUT + b, D, 3), :] = grad[:, b * LANES : (b + 1) * LANES]
    for i in (BO, G2, S2, BD):
        put_vector(i, gvec[i : i + 1, :])
    pack(range(early, n))
    for p in range(PARTS):
        reduce_start(p, 0, 1)
    gather_back(masks, res_s)
    emit_rows(img_v)
    out_copy = pltpu.make_async_copy(img_v, out_ref, load_sem.at[2])
    out_copy.start()

    def attend_back(t):
        rows, (cq, ck, cv) = views(t)
        q, k, v = qkv_s[rows, cq], qkv_s[rows, ck], qkv_s[rows, cv]
        dm = stack(ffn_s[rows, cq])
        probs = probs_s[t]
        wide = probs.astype(F32)
        dprobs = nt(dm, v)
        delta_p = jnp.sum(wide * dprobs, axis=-1, keepdims=True)
        ds = (wide * (dprobs - delta_p)).astype(BF)
        dvalue = tn(probs, dm)
        dq = nn(ds, k)
        dquery = jnp.where(low, dq[:tokp], dq[tokp:]) * (HD**-0.5)
        dkey = tn(ds, stack(q, HD**-0.5))
        gvec[BQ : BQ + 1, cq] += colsum(dquery)
        gvec[BV : BV + 1, cq] += colsum(dvalue)
        qkv_s[rows, cq] = dquery.astype(BF)
        qkv_s[rows, ck] = dkey.astype(BF)
        qkv_s[rows, cv] = dvalue.astype(BF)

    def backward(i, carry):
        for s in range(bits):
            @pl.when(i == ((s + 1) * trips) // (bits + 1))
            def _():
                reduce_round(s, 1)

        for u in range(UNROLL):
            attend_back(i * UNROLL + u)
        return carry

    lax.fori_loop(0, trips, backward, 0)

    def first_norm_back(i, carry):
        rows = band(i)
        dn1 = nt(qkv_s[rows, :], wqkv[...])
        hat1, inv1 = norm_stats(x_s[rows, :].astype(F32))
        add_vector(G1, colsum(dn1 * hat1))
        add_vector(S1, colsum(dn1))
        res_s[rows, :] = dn2_s[rows, :] + norm_back(dn1, hat1, inv1, param(G1))
        return carry

    lax.fori_loop(0, BLOCKS, first_norm_back, 0)

    def grad_qkv(c, carry):
        cols = pl.ds(pl.multiple_of(c * LANES, LANES), LANES)
        grad = tn(attn_s[:, cols], qkv_s[...])
        for b in range(9):
            at = 3 * ROW_QKV + 9 * LANES * c + b
            buf[pl.ds(at, LANES, 9), :] = grad[:, b * LANES : (b + 1) * LANES]
        return carry

    lax.fori_loop(0, 3, grad_qkv, 0)
    for i in (G1, S1, BQ, BV):
        put_vector(i, gvec[i : i + 1, :])
    pack(range(early))
    for p in range(PARTS):
        reduce_start(p, 0, 0)
    gather_back(None, res_s)
    emit_rows(cot_v)
    din_copy = pltpu.make_async_copy(cot_v, din_ref, load_sem.at[3])
    din_copy.start()
    for s in range(bits):
        reduce_round(s, 0)
    for wave in range(2):
        for p in range(PARTS):
            for s in range(bits):
                reduce_sent(p, s, wave)
    out_copy.wait()
    din_copy.wait()


def run_step(n, shard, window, live, mine, images, cotangent):
    tok, slots, _ = images.shape
    tokp = up_to(tok, 16)
    rows = slots * tokp
    flat = (slots * tok, D)
    buf_rows = up_to(max(shard * (n - 1) // LANES + window, 3 * ROWS) + 8, 8)
    whole = pl.BlockSpec(memory_space=pltpu.VMEM)
    apart = pl.BlockSpec(memory_space=pl.ANY)
    VM = pltpu.VMEM
    sems = pltpu.SemaphoreType.DMA((PARTS, n - 1))
    out, din, mine = pl.pallas_call(
        functools.partial(step_kernel, n, shard, slots, tok, tokp),
        in_specs=[pl.BlockSpec(memory_space=pltpu.SMEM), whole, apart, apart],
        out_specs=[apart, apart, whole],
        out_shape=[
            jax.ShapeDtypeStruct(flat, BF),
            jax.ShapeDtypeStruct(flat, BF),
            jax.ShapeDtypeStruct((window, LANES), F32),
        ],
        scratch_shapes=[
            VM((n, window, LANES), BF),
            VM((PARTS, n - 1, window // PARTS, LANES), BF),
            VM((buf_rows, LANES), F32),
            VM((D, 3 * D), BF), VM((D, D), BF), VM((D, FF), BF), VM((FF, D), BF),
            VM((8, D), F32), VM((1, FF), F32), VM((8, D), F32),
            VM(flat, BF), VM(flat, BF), VM((3, slots * tok, LANES), F32),
            VM((rows, D), BF), VM((rows, D), BF), VM((rows, D), BF),
            VM((rows, 3 * D), BF), VM((slots * PAIRS, 2 * tokp, tokp), BF),
            VM((rows, D), BF),
            VM((rows, D), F32), VM((rows, 1), F32), VM((rows, D), F32), VM((rows, D), F32), VM((rows, D), BF),
            pltpu.SemaphoreType.DMA((4,)), sems, sems, sems, sems,
        ],
        compiler_params=pltpu.CompilerParams(
            collective_id=1, has_side_effects=True, vmem_limit_bytes=67043328
        ),
        name="step",
    )(live, mine, images.reshape(flat), cotangent.reshape(flat))
    return out.reshape(tok, slots, D), din.reshape(tok, slots, D), mine


def shards(params, images, cotangent, live):
    n = lax.axis_size("dp")
    assert n & (n - 1) == 0 and n >= 4
    shard = params.shape[0]
    window = up_to((shard + 2 * LANES - 2) // LANES, 16 * PARTS)
    me = lax.axis_index("dp")
    shift = (shard % LANES) * me % LANES
    padded = jnp.pad(params, (0, window * LANES - shard))
    moved = jnp.roll(padded, shift).astype(BF).reshape(window, LANES)
    images, cotangent = (jnp.transpose(a, (1, 0, 2)) for a in (images, cotangent))
    out, din, mine = run_step(n, shard, window, live, moved, images, cotangent)
    out, din = (jnp.transpose(a, (1, 0, 2)) for a in (out, din))
    flat = lax.dynamic_slice(mine.reshape(-1), (shift,), (shard,))
    return out, din, flat


def solution(mesh):
    return jax.shard_map(
        shards,
        mesh=mesh,
        in_specs=(P("dp"), P("dp", None, None), P("dp", None, None), P("dp")),
        out_specs=(P("dp", None, None), P("dp", None, None), P("dp")),
        check_vma=False,
    )
```

```python
import functools

import jax
import jax.numpy as jnp
from jax import lax
from jax.experimental import pallas as pl
from jax.experimental.pallas import tpu as pltpu
from jax.sharding import PartitionSpec as P

D = 384
HEADS = 6
FF = 1536
HD = D // HEADS
PAIRS = HEADS // 2
EPS = 1e-06
LANES = 128
BF = jnp.bfloat16
F32 = jnp.float32

ROW_QKV = 2
ROW_OUT = 2 + 3 * D + 2
ROW_UP = ROW_OUT + D + 3
ROW_BUP = ROW_UP + FF
ROW_DOWN = ROW_BUP + FF // D
ROW_BDOWN = ROW_DOWN + FF
ROWS = ROW_BDOWN + 1
VEC_ROWS = (0, 1, ROW_OUT - 2, ROW_OUT - 1, ROW_UP - 3, ROW_UP - 2, ROW_UP - 1, ROW_BDOWN)
G1, S1, BQ, BV, BO, G2, S2, BD = range(8)

CHUNK = 256
PARTS = 4
UNROLL = 2
BLOCKS = 4
MESH = pl.DeviceIdType.MESH


def up_to(value, unit):
    return (value + unit - 1) // unit * unit


def nt(a, b):
    return lax.dot_general(a, b, (((1,), (1,)), ((), ())), preferred_element_type=F32)


def tn(a, b):
    return lax.dot_general(a, b, (((0,), (0,)), ((), ())), preferred_element_type=F32)


def nn(a, b):
    return jnp.dot(a, b, preferred_element_type=F32)


def norm_stats(values):
    center = values - jnp.mean(values, axis=-1, keepdims=True)
    inv = lax.rsqrt(jnp.mean(center * center, axis=-1, keepdims=True) + EPS)
    return center * inv, inv


def norm_back(grad_out, hat, inv, gain):
    g = grad_out * gain
    return inv * (
        g
        - jnp.mean(g, axis=-1, keepdims=True)
        - hat * jnp.mean(g * hat, axis=-1, keepdims=True)
    )


def colsum(v):
    return jnp.sum(v, axis=0, keepdims=True)


def low_orders(low_bits):
    near = list(range(low_bits))[::-1]
    swapped = near[1:2] + near[:1] + near[2:] if low_bits > 2 else near
    return [near, swapped] * (PARTS // 2)


def place(low, order):
    return sum((low >> b & 1) << i for i, b in enumerate(order))


def plan(n, shard):
    needed = -(-3 * ROW_OUT * LANES // shard)
    low_bits = max(needed.bit_length() - 1, 1)
    if needed > (1 << low_bits) + 1:
        low_bits += 1
    low_bits = min(low_bits, n.bit_length() - 2)
    head = 3 * ROW_OUT - (shard << low_bits) // LANES
    assert head <= 16
    return low_bits, max(head, 0)


def matrices():
    return (
        (0, D, 9, ROW_QKV),
        (1, D, 3, ROW_OUT),
        (2, D, 12, ROW_UP),
        (3, FF, 3, ROW_DOWN),
    )


def step_kernel(
    n, shard, slots, tok, tokp,
    live_ref, mine_ref, img_hbm, cot_hbm,
    out_ref, din_ref, flat_ref,
    gath, recv, recv_up, head_v, head_in, buf, wqkv, wout, wup, wdn, vec, bup, gvec,
    img_v, cot_v, stage, x_s, dout_s, attn_s, qkv_s, probs_s, mixed_s,
    hat_s, inv_s, res_s, dn2_s, ffn_s,
    load_sem, gu_send, gu_recv, gl_send, gl_recv,
    ru_send, ru_recv, rl_send, rl_recv, gh_send, gh_recv, rh_send, rh_recv,
):
    bits = n.bit_length() - 1
    me = lax.axis_index("dp")
    window = mine_ref.shape[0]
    part = window // PARTS
    weights = (wqkv, wout, wup, wdn)
    delta = [(1 - 2 * (me // (1 << b) % 2)) * (1 << b) for b in range(bits)]
    bit = [me // (1 << b) % 2 for b in range(bits)]
    e, head = plan(n, shard)
    near_count, uppers = 1 << e, n >> e
    up = me // near_count
    near_me = me % near_count
    orders = low_orders(e)
    spots = [sum(bit[b] * (1 << i) for i, b in enumerate(order)) for order in orders]
    waves = (pl.ds(0, 1), pl.ds(1, uppers - 1))

    def peer(j):
        return me + sum(delta[e + b] for b in range(bits - e) if j >> b & 1)

    def fixed(p, i):
        return sum(bit[b] * (1 << k) for k, b in enumerate(orders[p]) if k >= i)

    def remote(src, dst, send, recv_at, to):
        return pltpu.make_async_remote_copy(
            src_ref=src, dst_ref=dst, send_sem=send, recv_sem=recv_at,
            device_id=(to,), device_id_type=MESH,
        )

    def gather_upper(p, j):
        return remote(
            mine_ref.at[pl.ds(p * part, part)], gath.at[p, spots[p], up],
            gu_send.at[p, j - 1], gu_recv.at[p, j - 1], peer(j),
        )

    def gather_low(p, i, wave):
        held = gath.at[p, pl.ds(fixed(p, i), 1 << i), waves[wave]]
        return remote(
            held, held, gl_send.at[wave, p, i], gl_recv.at[wave, p, i],
            me + delta[orders[p][i]],
        )

    def send_own():
        for p in range(PARTS):
            for j in range(1, uppers):
                gather_upper(p, j).start()

    def gather_upper_arrive(p, wave):
        own = gath.at[p, spots[p], up]
        if wave == 0:
            @pl.when(up > 0)
            def _():
                remote(own, own, gu_send.at[p, 0], gu_recv.at[p, up - 1], me).wait_recv()
        else:
            for j in range(1, uppers):
                @pl.when(up != j)
                def _():
                    remote(own, own, gu_send.at[p, 0], gu_recv.at[p, j - 1], me).wait_recv()
        gather_low(p, 0, wave).start()

    def gather_round(i, wave):
        for p in range(PARTS):
            gather_low(p, i, wave).wait_recv()
            if i + 1 < e:
                gather_low(p, i + 1, wave).start()

    def zero_from(i):
        return sum(bit[b] for b in orders[0][i:]) if i < e else 0

    def head_gather_upper(wait):
        if wait:
            @pl.when(zero_from(0) + (up == 1).astype(jnp.int32) == 0)
            def _():
                at = up + 1 - 2 * (up % 2) - 1
                remote(head_v, head_v, gh_send.at[0], gh_recv.at[at], me).wait_recv()
        else:
            @pl.when(me == near_count)
            def _():
                head_v[...] = mine_ref[0:16, :]
                for j in range(1, uppers):
                    remote(
                        mine_ref.at[0:16], head_v, gh_send.at[j - 1], gh_recv.at[j - 1], peer(j)
                    ).start()

    def head_gather_low(i, wait):
        at = uppers - 1 + i
        copy = remote(head_v, head_v, gh_send.at[at], gh_recv.at[at], me + delta[orders[0][i]])
        if wait:
            @pl.when(zero_from(i + 1) * 2 + bit[orders[0][i]] == 1)
            def _():
                copy.wait_recv()
        else:
            @pl.when(zero_from(i) == 0)
            def _():
                copy.start()

    def gather_sent():
        for p in range(PARTS):
            for j in range(1, uppers):
                gather_upper(p, j).wait_send()
            for i in range(e):
                for wave in range(2):
                    gather_low(p, i, wave).wait_send()
        if head:
            @pl.when(me == near_count)
            def _():
                for j in range(1, uppers):
                    remote(
                        mine_ref.at[0:16], head_v, gh_send.at[j - 1], gh_recv.at[j - 1], peer(j)
                    ).wait_send()
            for i in range(e):
                @pl.when(zero_from(i) == 0)
                def _():
                    at = uppers - 1 + i
                    remote(
                        head_v, head_v, gh_send.at[at], gh_recv.at[at], me + delta[orders[0][i]]
                    ).wait_send()

    def reduce_low(p, i, wave):
        other = fixed(p, i + 1) + (1 - bit[orders[p][i]]) * (1 << i)
        return remote(
            gath.at[p, pl.ds(other, 1 << i), waves[wave]],
            recv.at[p, pl.ds((1 << i) - 1, 1 << i), waves[wave]],
            rl_send.at[wave, p, i], rl_recv.at[wave, p, i], me + delta[orders[p][i]],
        )

    def reduce_upper(p, j, block, to):
        return remote(
            gath.at[p, spots[p], block], recv_up.at[p, j - 1],
            ru_send.at[p, j - 1], ru_recv.at[p, j - 1], to,
        )

    def reduce_upper_start(p, wave):
        if wave == 0:
            @pl.when(up > 0)
            def _():
                reduce_upper(p, up, 0, near_me).start()
        else:
            for j in range(1, uppers):
                @pl.when(up != j)
                def _():
                    reduce_upper(p, j, peer(j) // near_count, peer(j)).start()

    def reduce_round(i, wave):
        for p in range(PARTS):
            reduce_low(p, i, wave).wait_recv()
            keep = pl.ds(fixed(p, i), 1 << i)
            slot = pl.ds((1 << i) - 1, 1 << i)
            total = gath[p, keep, waves[wave]].astype(F32) + recv[p, slot, waves[wave]].astype(F32)
            gath[p, keep, waves[wave]] = total.astype(BF)
            if i > 0:
                reduce_low(p, i - 1, wave).start()
            else:
                reduce_upper_start(p, wave)

    def reduce_last(wave):
        @pl.when(up == 0 if wave == 0 else up > 0)
        def _():
            for p in range(PARTS):
                total = gath[p, spots[p], up].astype(F32)
                for j in range(1, uppers):
                    reduce_upper(p, j, 0, me).wait_recv()
                    total = total + recv_up[p, j - 1].astype(F32)
                flat_ref[p * part : (p + 1) * part, :] = total

    def head_reduce_low(i):
        copy = remote(
            head_v, head_in.at[i], rh_send.at[0], rh_recv.at[i], me + delta[orders[0][i]]
        )

        @pl.when(zero_from(i + 1) * 2 + bit[orders[0][i]] == 1)
        def _():
            copy.start()
            copy.wait_send()

        @pl.when(zero_from(i) == 0)
        def _():
            copy.wait_recv()
            head_v[...] = (head_v[...].astype(F32) + head_in[i].astype(F32)).astype(BF)

    def head_reduce_upper():
        @pl.when(zero_from(0) + (up == 1).astype(jnp.int32) == 0)
        def _():
            at = up + 1 - 2 * (up % 2) - 1
            copy = remote(head_v, head_in.at[e + at], rh_send.at[0], rh_recv.at[e + at], near_count)
            copy.start()
            copy.wait_send()

        @pl.when(me == near_count)
        def _():
            total = head_v[...].astype(F32)
            for j in range(1, uppers):
                at = e + j - 1
                remote(head_v, head_in.at[at], rh_send.at[0], rh_recv.at[at], me).wait_recv()
                total = total + head_in[at].astype(F32)
            flat_ref[0:16, :] = total

    def reduce_sent():
        for p in range(PARTS):
            for j in range(1, uppers):
                reduce_upper(p, j, 0, me).wait_send()
            for i in range(e):
                for wave in range(2):
                    reduce_low(p, i, wave).wait_send()

    def home(d, p):
        return p, place(d % near_count, orders[p]), d // near_count

    def unpack(blocks):
        for d in blocks:
            first, shift = divmod(shard * d, LANES)
            rows = (shift + shard + LANES - 1) // LANES
            for p in range(PARTS):
                count = min(part, rows - p * part)
                if count <= 0:
                    break
                at = first + p * part
                piece = gath[home(d, p)].astype(F32)
                if d > 0 and shift and p == 0:
                    seam = buf[at : at + 1, :] + piece[0:1]
                    buf[at : at + count, :] = piece[:count]
                    buf[at : at + 1, :] = seam
                else:
                    buf[at : at + count, :] = piece[:count]

    def unpack_head():
        first, shift = divmod(shard * near_count, LANES)
        piece = head_v[...].astype(F32)
        if shift:
            piece = piece + jnp.where(
                lax.broadcasted_iota(jnp.int32, piece.shape, 0) == 0, buf[first : first + 16, :], 0.0
            )
        buf[first : first + 16, :] = piece

    def load_matrix(k, rows, blocks, start):
        for b in range(blocks):
            weights[k][:, b * LANES : (b + 1) * LANES] = buf[
                pl.ds(3 * start + b, rows, blocks), :
            ].astype(BF)

    def load_vectors(indices):
        for i in indices:
            r = VEC_ROWS[i]
            for c in range(3):
                vec[i : i + 1, c * LANES : (c + 1) * LANES] = buf[3 * r + c : 3 * r + c + 1, :]

    def put_vector(i, value):
        r = VEC_ROWS[i]
        for c in range(3):
            buf[3 * r + c : 3 * r + c + 1, :] = value[:, c * LANES : (c + 1) * LANES]

    def pack(blocks):
        for d in blocks:
            first = shard * d // LANES
            for p in range(PARTS):
                at = first + p * part
                gath[home(d, p)] = buf[at : at + part, :].astype(BF)

    def param(i):
        return vec[i : i + 1, :]

    loads = [
        pltpu.make_async_copy(img_hbm, img_v, load_sem.at[0]),
        pltpu.make_async_copy(cot_hbm, cot_v, load_sem.at[1]),
    ]
    for c in loads:
        c.start()
    partners = [me + delta[b] for b in range(e)] + [peer(j) for j in range(1, uppers)]
    barrier = pltpu.get_barrier_semaphore()
    for partner in partners:
        pl.semaphore_signal(barrier, inc=1, device_id=(partner,), device_id_type=MESH)
    pl.semaphore_wait(barrier, len(partners))

    @pl.when(up == 0)
    def _():
        send_own()

    if head:
        head_gather_upper(False)
    for p in range(PARTS):
        gath[p, spots[p], up] = mine_ref[p * part : (p + 1) * part, :]

    def scatter_rows(source, target, scales):
        for c in range(3):
            stage[c] = source[:, c * LANES : (c + 1) * LANES].astype(F32)
        target[...] = jnp.zeros_like(target)
        for g in range(slots):
            for c in range(3):
                cols = slice(c * LANES, (c + 1) * LANES)
                v = stage[c, pl.ds(g, tok, slots), :]
                if scales is not None:
                    v = v * scales[g]
                target[g * tokp : g * tokp + tok, cols] = v.astype(BF)

    live = live_ref[0]
    masks = [(g < live).astype(F32) for g in range(slots)]
    loads[0].wait()
    scatter_rows(img_v, x_s, None)
    for p in range(PARTS):
        gather_upper_arrive(p, 0)

    @pl.when(up > 0)
    def _():
        send_own()

    if head:
        head_gather_upper(True)
    loads[1].wait()
    if head:
        head_gather_low(0, False)
    scatter_rows(cot_v, dout_s, masks)
    for i in range(e):
        gather_round(i, 0)
        if head:
            head_gather_low(i, True)
            if i + 1 < e:
                head_gather_low(i + 1, False)
    unpack(range(near_count))
    if head:
        unpack_head()
    load_matrix(*matrices()[0])
    load_vectors((G1, S1, BQ, BV))
    gvec[...] = jnp.zeros_like(gvec)

    height = x_s.shape[0] // BLOCKS
    bias = jnp.concatenate([param(BQ), jnp.zeros((1, D), F32), param(BV)], axis=1)

    def band(i):
        return pl.ds(pl.multiple_of(i * height, 16), height)

    def project(i, carry):
        hat1, _ = norm_stats(x_s[band(i), :].astype(F32))
        attn_in = (hat1 * param(G1) + param(S1)).astype(BF)
        attn_s[band(i), :] = attn_in
        qkv_s[band(i), :] = (nn(attn_in, wqkv[...]) + bias).astype(BF)
        return carry

    lax.fori_loop(0, BLOCKS, project, 0)

    lane = lax.broadcasted_iota(jnp.int32, (1, LANES), 1)
    low = lane < HD
    low_b = low.astype(BF)
    high_b = 1 - low_b
    key_ok = lax.broadcasted_iota(jnp.int32, (1, tokp), 1) < tok

    def views(t):
        g, p = t // PAIRS, t % PAIRS
        rows = pl.ds(pl.multiple_of(g * tokp, 16), tokp)
        return rows, [pl.ds(pl.multiple_of(j * D + p * LANES, LANES), LANES) for j in range(3)]

    def stack(v, scale=1.0):
        return jnp.concatenate([v * (low_b * scale), v * (high_b * scale)], axis=0)

    def attend(t):
        rows, (cq, ck, cv) = views(t)
        q, k, v = qkv_s[rows, cq], qkv_s[rows, ck], qkv_s[rows, cv]
        s = nt(stack(q, HD**-0.5), k)
        s = jnp.where(key_ok, s, -1e30)
        e = jnp.exp(s - jnp.max(s, axis=-1, keepdims=True))
        probs = (e * (1.0 / jnp.sum(e, axis=-1, keepdims=True))).astype(BF)
        probs_s[t] = probs
        mixed = nn(probs, v)
        mixed_s[rows, cq] = jnp.where(low, mixed[:tokp], mixed[tokp:]).astype(BF)

    tiles = slots * PAIRS
    trips = tiles // UNROLL

    def forward(i, carry):
        for r in range(e + 1):
            @pl.when(i == (r * trips) // (e + 1))
            def _():
                if r == 0:
                    for p in range(PARTS):
                        gather_upper_arrive(p, 1)
                else:
                    gather_round(r - 1, 1)

        for u in range(UNROLL):
            attend(i * UNROLL + u)
        return carry

    lax.fori_loop(0, trips, forward, 0)
    gather_sent()
    unpack(range(near_count, n))
    for m in matrices()[1:]:
        load_matrix(*m)
    load_vectors((BO, G2, S2, BD))
    for c in range(FF // LANES):
        bup[:, c * LANES : (c + 1) * LANES] = buf[3 * ROW_BUP + c : 3 * ROW_BUP + c + 1, :]
    tail = buf.shape[0] - 3 * ROWS
    buf[3 * ROWS :, :] = jnp.zeros((tail, LANES), F32)

    def add_vector(i, value):
        gvec[i : i + 1, :] += value

    def second_norm(i, carry):
        rows = band(i)
        hidden = x_s[rows, :].astype(F32) + nn(mixed_s[rows, :], wout[...]) + param(BO)
        hat2, inv2 = norm_stats(hidden)
        ffn_s[rows, :] = (hat2 * param(G2) + param(S2)).astype(BF)
        hat_s[rows, :] = hat2
        inv_s[rows, :] = inv2
        res_s[rows, :] = hidden + param(BD)
        dn2_s[rows, :] = jnp.zeros((height, D), F32)
        add_vector(BD, colsum(dout_s[rows, :].astype(F32)))
        return carry

    lax.fori_loop(0, BLOCKS, second_norm, 0)

    def feed(c, carry):
        cols = pl.ds(pl.multiple_of(c * CHUNK, CHUNK), CHUNK)
        ffn_in = ffn_s[...]
        dout_b = dout_s[...]
        pre = nn(ffn_in, wup[:, cols]) + bup[:, cols]
        cumul = 0.5 * (1.0 + lax.erf(pre * 0.7071067811865476))
        act = (pre * cumul).astype(BF)
        res_s[...] += nn(act, wdn[cols, :])
        grad = tn(act, dout_b)
        for b in range(3):
            buf[pl.ds(3 * ROW_DOWN + 3 * CHUNK * c + b, CHUNK, 3), :] = grad[
                :, b * LANES : (b + 1) * LANES
            ]
        density = jnp.exp(-0.5 * pre * pre) * 0.3989422804014327
        dpre = nt(dout_b, wdn[cols, :]) * (cumul + pre * density)
        total = colsum(dpre)
        dpre_b = dpre.astype(BF)
        grad = tn(ffn_in, dpre_b)
        for b in range(CHUNK // LANES):
            lanes = slice(b * LANES, (b + 1) * LANES)
            at = c * (CHUNK // LANES) + b
            buf[pl.ds(3 * ROW_UP + at, D, FF // LANES), :] = grad[:, lanes]
            buf[pl.ds(3 * ROW_BUP + at, 1), :] = total[:, lanes]
        dn2_s[...] += nt(dpre_b, wup[:, cols])
        return carry

    lax.fori_loop(0, FF // CHUNK, feed, 0)

    def gather_back(value, source_ref):
        for g in range(slots):
            for c in range(3):
                cols = slice(c * LANES, (c + 1) * LANES)
                v = source_ref[g * tokp : g * tokp + tok, cols]
                if value is not None:
                    v = v * value[g]
                stage[c, pl.ds(g, tok, slots), :] = v

    def emit_rows(target):
        for c in range(3):
            target[:, c * LANES : (c + 1) * LANES] = stage[c].astype(BF)

    def second_norm_back(i, carry):
        rows = band(i)
        hat2 = hat_s[rows, :]
        dn2 = dn2_s[rows, :]
        add_vector(G2, colsum(dn2 * hat2))
        add_vector(S2, colsum(dn2))
        dhidden = dout_s[rows, :].astype(F32) + norm_back(dn2, hat2, inv_s[rows, :], param(G2))
        dn2_s[rows, :] = dhidden
        dhidden_b = dhidden.astype(BF)
        add_vector(BO, colsum(dhidden))
        dout_s[rows, :] = dhidden_b
        ffn_s[rows, :] = nt(dhidden_b, wout[...]).astype(BF)
        return carry

    lax.fori_loop(0, BLOCKS, second_norm_back, 0)
    grad = tn(mixed_s[...], dout_s[...])
    for b in range(3):
        buf[pl.ds(3 * ROW_OUT + b, D, 3), :] = grad[:, b * LANES : (b + 1) * LANES]
    for i in (BO, G2, S2, BD):
        put_vector(i, gvec[i : i + 1, :])
    pack(range(near_count, n))
    for p in range(PARTS):
        reduce_low(p, e - 1, 1).start()
    gather_back(masks, res_s)
    emit_rows(img_v)
    out_copy = pltpu.make_async_copy(img_v, out_ref, load_sem.at[2])
    out_copy.start()

    def attend_back(t):
        rows, (cq, ck, cv) = views(t)
        q, k, v = qkv_s[rows, cq], qkv_s[rows, ck], qkv_s[rows, cv]
        dm = stack(ffn_s[rows, cq])
        probs = probs_s[t]
        wide = probs.astype(F32)
        dprobs = nt(dm, v)
        delta_p = jnp.sum(wide * dprobs, axis=-1, keepdims=True)
        ds = (wide * (dprobs - delta_p)).astype(BF)
        dvalue = tn(probs, dm)
        dq = nn(ds, k)
        dquery = jnp.where(low, dq[:tokp], dq[tokp:]) * (HD**-0.5)
        dkey = tn(ds, stack(q, HD**-0.5))
        gvec[BQ : BQ + 1, cq] += colsum(dquery)
        gvec[BV : BV + 1, cq] += colsum(dvalue)
        qkv_s[rows, cq] = dquery.astype(BF)
        qkv_s[rows, ck] = dkey.astype(BF)
        qkv_s[rows, cv] = dvalue.astype(BF)

    def backward(i, carry):
        for r in range(e + 1):
            @pl.when(i == ((r + 1) * trips) // (e + 2))
            def _():
                if r < e:
                    reduce_round(e - 1 - r, 1)
                else:
                    reduce_last(1)

        for u in range(UNROLL):
            attend_back(i * UNROLL + u)
        return carry

    lax.fori_loop(0, trips, backward, 0)

    def first_norm_back(i, carry):
        rows = band(i)
        dn1 = nt(qkv_s[rows, :], wqkv[...])
        hat1, inv1 = norm_stats(x_s[rows, :].astype(F32))
        add_vector(G1, colsum(dn1 * hat1))
        add_vector(S1, colsum(dn1))
        res_s[rows, :] = dn2_s[rows, :] + norm_back(dn1, hat1, inv1, param(G1))
        return carry

    lax.fori_loop(0, BLOCKS, first_norm_back, 0)

    def grad_qkv(c, carry):
        cols = pl.ds(pl.multiple_of(c * LANES, LANES), LANES)
        grad = tn(attn_s[:, cols], qkv_s[...])
        for b in range(9):
            at = 3 * ROW_QKV + 9 * LANES * c + b
            buf[pl.ds(at, LANES, 9), :] = grad[:, b * LANES : (b + 1) * LANES]
        return carry

    lax.fori_loop(0, 3, grad_qkv, 0)
    for i in (G1, S1, BQ, BV):
        put_vector(i, gvec[i : i + 1, :])
    pack(range(near_count))
    for p in range(PARTS):
        reduce_low(p, e - 1, 0).start()
    if head:
        at = shard * near_count // LANES
        head_v[...] = buf[at : at + 16, :].astype(BF)
    gather_back(None, res_s)
    emit_rows(cot_v)
    din_copy = pltpu.make_async_copy(cot_v, din_ref, load_sem.at[3])
    din_copy.start()
    for i in reversed(range(e)):
        reduce_round(i, 0)
        if head:
            head_reduce_low(i)
    if head:
        head_reduce_upper()
    reduce_last(0)
    reduce_sent()
    out_copy.wait()
    din_copy.wait()


def run_step(n, shard, window, live, mine, images, cotangent):
    tok, slots, _ = images.shape
    tokp = up_to(tok, 16)
    rows = slots * tokp
    flat = (slots * tok, D)
    buf_rows = up_to(max(shard * (n - 1) // LANES + window, 3 * ROWS) + 8, 8)
    whole = pl.BlockSpec(memory_space=pltpu.VMEM)
    apart = pl.BlockSpec(memory_space=pl.ANY)
    VM = pltpu.VMEM
    e, _ = plan(n, shard)
    near_count, uppers = 1 << e, n >> e
    part = window // PARTS
    DMA = pltpu.SemaphoreType.DMA
    across = DMA((PARTS, uppers - 1))
    inside = DMA((2, PARTS, e))
    tops = DMA((uppers - 1 + e,))
    out, din, mine = pl.pallas_call(
        functools.partial(step_kernel, n, shard, slots, tok, tokp),
        in_specs=[pl.BlockSpec(memory_space=pltpu.SMEM), whole, apart, apart],
        out_specs=[apart, apart, whole],
        out_shape=[
            jax.ShapeDtypeStruct(flat, BF),
            jax.ShapeDtypeStruct(flat, BF),
            jax.ShapeDtypeStruct((window, LANES), F32),
        ],
        scratch_shapes=[
            VM((PARTS, near_count, uppers, part, LANES), BF),
            VM((PARTS, near_count - 1, uppers, part, LANES), BF),
            VM((PARTS, uppers - 1, part, LANES), BF),
            VM((16, LANES), BF), VM((e + uppers - 1, 16, LANES), BF),
            VM((buf_rows, LANES), F32),
            VM((D, 3 * D), BF), VM((D, D), BF), VM((D, FF), BF), VM((FF, D), BF),
            VM((8, D), F32), VM((1, FF), F32), VM((8, D), F32),
            VM(flat, BF), VM(flat, BF), VM((3, slots * tok, LANES), F32),
            VM((rows, D), BF), VM((rows, D), BF), VM((rows, D), BF),
            VM((rows, 3 * D), BF), VM((slots * PAIRS, 2 * tokp, tokp), BF),
            VM((rows, D), BF),
            VM((rows, D), F32), VM((rows, 1), F32), VM((rows, D), F32), VM((rows, D), F32), VM((rows, D), BF),
            DMA((4,)), across, across, inside, inside, across, across, inside, inside,
            tops, tops, DMA((1,)), tops,
        ],
        compiler_params=pltpu.CompilerParams(
            collective_id=1, has_side_effects=True, vmem_limit_bytes=67043328
        ),
        name="step",
    )(live, mine, images.reshape(flat), cotangent.reshape(flat))
    return out.reshape(tok, slots, D), din.reshape(tok, slots, D), mine


def shards(params, images, cotangent, live):
    n = lax.axis_size("dp")
    assert n & (n - 1) == 0 and n >= 4
    shard = params.shape[0]
    window = up_to((shard + 2 * LANES - 2) // LANES, 16 * PARTS)
    me = lax.axis_index("dp")
    shift = (shard % LANES) * me % LANES
    padded = jnp.pad(params, (0, window * LANES - shard))
    moved = jnp.roll(padded, shift).astype(BF).reshape(window, LANES)
    images, cotangent = (jnp.transpose(a, (1, 0, 2)) for a in (images, cotangent))
    out, din, mine = run_step(n, shard, window, live, moved, images, cotangent)
    out, din = (jnp.transpose(a, (1, 0, 2)) for a in (out, din))
    flat = lax.dynamic_slice(mine.reshape(-1), (shift,), (shard,))
    return out, din, flat


def solution(mesh):
    return jax.shard_map(
        shards,
        mesh=mesh,
        in_specs=(P("dp"), P("dp", None, None), P("dp", None, None), P("dp")),
        out_specs=(P("dp", None, None), P("dp", None, None), P("dp")),
        check_vma=False,
    )
```

```python
import functools

import jax
import jax.numpy as jnp
from jax import lax
from jax.experimental import pallas as pl
from jax.experimental.pallas import tpu as pltpu
from jax.sharding import PartitionSpec as P

D = 384
HEADS = 6
FF = 1536
HD = D // HEADS
PAIRS = HEADS // 2
EPS = 1e-06
LANES = 128
BF = jnp.bfloat16
F32 = jnp.float32

ROW_QKV = 2
ROW_OUT = 2 + 3 * D + 2
ROW_UP = ROW_OUT + D + 3
ROW_BUP = ROW_UP + FF
ROW_DOWN = ROW_BUP + FF // D
ROW_BDOWN = ROW_DOWN + FF
ROWS = ROW_BDOWN + 1
VEC_ROWS = (0, 1, ROW_OUT - 2, ROW_OUT - 1, ROW_UP - 3, ROW_UP - 2, ROW_UP - 1, ROW_BDOWN)
G1, S1, BQ, BV, BO, G2, S2, BD = range(8)

CHUNK = 512
PARTS = 4
UNROLL = 4
BLOCKS = 4
MESH = pl.DeviceIdType.MESH


def up_to(value, unit):
    return (value + unit - 1) // unit * unit


def nt(a, b):
    return lax.dot_general(a, b, (((1,), (1,)), ((), ())), preferred_element_type=F32)


def tn(a, b):
    return lax.dot_general(a, b, (((0,), (0,)), ((), ())), preferred_element_type=F32)


def nn(a, b):
    return jnp.dot(a, b, preferred_element_type=F32)


def norm_stats(values):
    center = values - jnp.mean(values, axis=-1, keepdims=True)
    inv = lax.rsqrt(jnp.mean(center * center, axis=-1, keepdims=True) + EPS)
    return center * inv, inv


def norm_back(grad_out, hat, inv, gain):
    g = grad_out * gain
    return inv * (
        g
        - jnp.mean(g, axis=-1, keepdims=True)
        - hat * jnp.mean(g * hat, axis=-1, keepdims=True)
    )


def colsum(v):
    return jnp.sum(v, axis=0, keepdims=True)


def low_orders(low_bits):
    near = list(range(low_bits))[::-1]
    swapped = near[1:2] + near[:1] + near[2:] if low_bits > 2 else near
    return [near, swapped] * (PARTS // 2)


def place(low, order):
    return sum((low >> b & 1) << i for i, b in enumerate(order))


def plan(n, shard):
    needed = -(-3 * ROW_OUT * LANES // shard)
    low_bits = max(needed.bit_length() - 1, 1)
    if needed > (1 << low_bits) + 1:
        low_bits += 1
    low_bits = min(low_bits, n.bit_length() - 2)
    head = 3 * ROW_OUT - (shard << low_bits) // LANES
    assert head <= 16
    return low_bits, max(head, 0)


def matrices():
    return (
        (0, D, 9, ROW_QKV),
        (1, D, 3, ROW_OUT),
        (2, D, 12, ROW_UP),
        (3, FF, 3, ROW_DOWN),
    )


def step_kernel(
    n, shard, slots, tok, tokp,
    live_ref, mine_ref, img_hbm, cot_hbm,
    out_ref, din_ref, flat_ref,
    gath, recv, recv_up, head_v, head_in, buf, wqkv, wout, wup, wdn, vec, bup, gvec,
    img_v, cot_v, stage, x_s, dout_s, attn_s, qkv_s, probs_s, mixed_s,
    hat_s, inv_s, res_s, dn2_s, ffn_s,
    load_sem, gu_send, gu_recv, gl_send, gl_recv,
    ru_send, ru_recv, rl_send, rl_recv, gh_send, gh_recv, rh_send, rh_recv,
):
    bits = n.bit_length() - 1
    me = lax.axis_index("dp")
    window = mine_ref.shape[0]
    part = window // PARTS
    weights = (wqkv, wout, wup, wdn)
    delta = [(1 - 2 * (me // (1 << b) % 2)) * (1 << b) for b in range(bits)]
    bit = [me // (1 << b) % 2 for b in range(bits)]
    e, head = plan(n, shard)
    near_count, uppers = 1 << e, n >> e
    up = me // near_count
    near_me = me % near_count
    orders = low_orders(e)
    spots = [sum(bit[b] * (1 << i) for i, b in enumerate(order)) for order in orders]
    waves = (pl.ds(0, 1), pl.ds(1, uppers - 1))

    def peer(j):
        return me + sum(delta[e + b] for b in range(bits - e) if j >> b & 1)

    def fixed(p, i):
        return sum(bit[b] * (1 << k) for k, b in enumerate(orders[p]) if k >= i)

    def remote(src, dst, send, recv_at, to):
        return pltpu.make_async_remote_copy(
            src_ref=src, dst_ref=dst, send_sem=send, recv_sem=recv_at,
            device_id=(to,), device_id_type=MESH,
        )

    def gather_upper(p, j):
        return remote(
            mine_ref.at[pl.ds(p * part, part)], gath.at[p, spots[p], up],
            gu_send.at[p, j - 1], gu_recv.at[p, j - 1], peer(j),
        )

    def gather_low(p, i, wave):
        held = gath.at[p, pl.ds(fixed(p, i), 1 << i), waves[wave]]
        return remote(
            held, held, gl_send.at[wave, p, i], gl_recv.at[wave, p, i],
            me + delta[orders[p][i]],
        )

    def send_own():
        for p in range(PARTS):
            for j in range(1, uppers):
                gather_upper(p, j).start()

    def gather_upper_arrive(p, wave):
        own = gath.at[p, spots[p], up]
        if wave == 0:
            @pl.when(up > 0)
            def _():
                remote(own, own, gu_send.at[p, 0], gu_recv.at[p, up - 1], me).wait_recv()
        else:
            for j in range(1, uppers):
                @pl.when(up != j)
                def _():
                    remote(own, own, gu_send.at[p, 0], gu_recv.at[p, j - 1], me).wait_recv()
        gather_low(p, 0, wave).start()

    def gather_round(i, wave):
        for p in range(PARTS):
            gather_low(p, i, wave).wait_recv()
            if i + 1 < e:
                gather_low(p, i + 1, wave).start()

    def zero_from(i):
        return sum(bit[b] for b in orders[0][i:]) if i < e else 0

    def head_gather_upper(wait):
        if wait:
            @pl.when(zero_from(0) + (up == 1).astype(jnp.int32) == 0)
            def _():
                at = up + 1 - 2 * (up % 2) - 1
                remote(head_v, head_v, gh_send.at[0], gh_recv.at[at], me).wait_recv()
        else:
            @pl.when(me == near_count)
            def _():
                head_v[...] = mine_ref[0:16, :]
                for j in range(1, uppers):
                    remote(
                        mine_ref.at[0:16], head_v, gh_send.at[j - 1], gh_recv.at[j - 1], peer(j)
                    ).start()

    def head_gather_low(i, wait):
        at = uppers - 1 + i
        copy = remote(head_v, head_v, gh_send.at[at], gh_recv.at[at], me + delta[orders[0][i]])
        if wait:
            @pl.when(zero_from(i + 1) * 2 + bit[orders[0][i]] == 1)
            def _():
                copy.wait_recv()
        else:
            @pl.when(zero_from(i) == 0)
            def _():
                copy.start()

    def gather_sent():
        for p in range(PARTS):
            for j in range(1, uppers):
                gather_upper(p, j).wait_send()
            for i in range(e):
                for wave in range(2):
                    gather_low(p, i, wave).wait_send()
        if head:
            @pl.when(me == near_count)
            def _():
                for j in range(1, uppers):
                    remote(
                        mine_ref.at[0:16], head_v, gh_send.at[j - 1], gh_recv.at[j - 1], peer(j)
                    ).wait_send()
            for i in range(e):
                @pl.when(zero_from(i) == 0)
                def _():
                    at = uppers - 1 + i
                    remote(
                        head_v, head_v, gh_send.at[at], gh_recv.at[at], me + delta[orders[0][i]]
                    ).wait_send()

    def reduce_low(p, i, wave):
        other = fixed(p, i + 1) + (1 - bit[orders[p][i]]) * (1 << i)
        return remote(
            gath.at[p, pl.ds(other, 1 << i), waves[wave]],
            recv.at[p, pl.ds((1 << i) - 1, 1 << i), waves[wave]],
            rl_send.at[wave, p, i], rl_recv.at[wave, p, i], me + delta[orders[p][i]],
        )

    def reduce_upper(p, j, block, to):
        return remote(
            gath.at[p, spots[p], block], recv_up.at[p, j - 1],
            ru_send.at[p, j - 1], ru_recv.at[p, j - 1], to,
        )

    def reduce_upper_start(p, wave):
        if wave == 0:
            @pl.when(up > 0)
            def _():
                reduce_upper(p, up, 0, near_me).start()
        else:
            for j in range(1, uppers):
                @pl.when(up != j)
                def _():
                    reduce_upper(p, j, peer(j) // near_count, peer(j)).start()

    def reduce_round(i, wave):
        for p in range(PARTS):
            reduce_low(p, i, wave).wait_recv()
            keep = pl.ds(fixed(p, i), 1 << i)
            slot = pl.ds((1 << i) - 1, 1 << i)
            total = gath[p, keep, waves[wave]].astype(F32) + recv[p, slot, waves[wave]].astype(F32)
            gath[p, keep, waves[wave]] = total.astype(BF)
            if i > 0:
                reduce_low(p, i - 1, wave).start()
            else:
                reduce_upper_start(p, wave)

    def reduce_last(wave):
        @pl.when(up == 0 if wave == 0 else up > 0)
        def _():
            for p in range(PARTS):
                total = gath[p, spots[p], up].astype(F32)
                for j in range(1, uppers):
                    reduce_upper(p, j, 0, me).wait_recv()
                    total = total + recv_up[p, j - 1].astype(F32)
                flat_ref[p * part : (p + 1) * part, :] = total

    def head_reduce_low(i):
        copy = remote(
            head_v, head_in.at[i], rh_send.at[0], rh_recv.at[i], me + delta[orders[0][i]]
        )

        @pl.when(zero_from(i + 1) * 2 + bit[orders[0][i]] == 1)
        def _():
            copy.start()
            copy.wait_send()

        @pl.when(zero_from(i) == 0)
        def _():
            copy.wait_recv()
            head_v[...] = (head_v[...].astype(F32) + head_in[i].astype(F32)).astype(BF)

    def head_reduce_upper():
        @pl.when(zero_from(0) + (up == 1).astype(jnp.int32) == 0)
        def _():
            at = up + 1 - 2 * (up % 2) - 1
            copy = remote(head_v, head_in.at[e + at], rh_send.at[0], rh_recv.at[e + at], near_count)
            copy.start()
            copy.wait_send()

        @pl.when(me == near_count)
        def _():
            total = head_v[...].astype(F32)
            for j in range(1, uppers):
                at = e + j - 1
                remote(head_v, head_in.at[at], rh_send.at[0], rh_recv.at[at], me).wait_recv()
                total = total + head_in[at].astype(F32)
            flat_ref[0:16, :] = total

    def reduce_sent():
        for p in range(PARTS):
            for j in range(1, uppers):
                reduce_upper(p, j, 0, me).wait_send()
            for i in range(e):
                for wave in range(2):
                    reduce_low(p, i, wave).wait_send()

    def home(d, p):
        return p, place(d % near_count, orders[p]), d // near_count

    def unpack(blocks):
        for d in blocks:
            first, shift = divmod(shard * d, LANES)
            rows = (shift + shard + LANES - 1) // LANES
            for p in range(PARTS):
                count = min(part, rows - p * part)
                if count <= 0:
                    break
                at = first + p * part
                piece = gath[home(d, p)].astype(F32)
                if d > 0 and shift and p == 0:
                    seam = buf[at : at + 1, :] + piece[0:1]
                    buf[at : at + count, :] = piece[:count]
                    buf[at : at + 1, :] = seam
                else:
                    buf[at : at + count, :] = piece[:count]

    def unpack_head():
        first, shift = divmod(shard * near_count, LANES)
        piece = head_v[...].astype(F32)
        if shift:
            piece = piece + jnp.where(
                lax.broadcasted_iota(jnp.int32, piece.shape, 0) == 0, buf[first : first + 16, :], 0.0
            )
        buf[first : first + 16, :] = piece

    def load_matrix(k, rows, blocks, start):
        for b in range(blocks):
            weights[k][:, b * LANES : (b + 1) * LANES] = buf[
                pl.ds(3 * start + b, rows, blocks), :
            ].astype(BF)

    def load_vectors(indices):
        for i in indices:
            r = VEC_ROWS[i]
            for c in range(3):
                vec[i : i + 1, c * LANES : (c + 1) * LANES] = buf[3 * r + c : 3 * r + c + 1, :]

    def put_vector(i, value):
        r = VEC_ROWS[i]
        for c in range(3):
            buf[3 * r + c : 3 * r + c + 1, :] = value[:, c * LANES : (c + 1) * LANES]

    def pack(blocks):
        for d in blocks:
            first = shard * d // LANES
            for p in range(PARTS):
                at = first + p * part
                gath[home(d, p)] = buf[at : at + part, :].astype(BF)

    def param(i):
        return vec[i : i + 1, :]

    loads = [
        pltpu.make_async_copy(img_hbm, img_v, load_sem.at[0]),
        pltpu.make_async_copy(cot_hbm, cot_v, load_sem.at[1]),
    ]
    for c in loads:
        c.start()
    partners = [me + delta[b] for b in range(e)] + [peer(j) for j in range(1, uppers)]
    barrier = pltpu.get_barrier_semaphore()
    for partner in partners:
        pl.semaphore_signal(barrier, inc=1, device_id=(partner,), device_id_type=MESH)
    pl.semaphore_wait(barrier, len(partners))

    @pl.when(up == 0)
    def _():
        send_own()

    if head:
        head_gather_upper(False)
    for p in range(PARTS):
        gath[p, spots[p], up] = mine_ref[p * part : (p + 1) * part, :]

    def scatter_rows(source, target, scales):
        for c in range(3):
            stage[c] = source[:, c * LANES : (c + 1) * LANES].astype(F32)
        target[...] = jnp.zeros_like(target)
        for g in range(slots):
            for c in range(3):
                cols = slice(c * LANES, (c + 1) * LANES)
                v = stage[c, pl.ds(g, tok, slots), :]
                if scales is not None:
                    v = v * scales[g]
                target[g * tokp : g * tokp + tok, cols] = v.astype(BF)

    live = live_ref[0]
    masks = [(g < live).astype(F32) for g in range(slots)]
    loads[0].wait()
    scatter_rows(img_v, x_s, None)
    for p in range(PARTS):
        gather_upper_arrive(p, 0)

    @pl.when(up > 0)
    def _():
        send_own()

    if head:
        head_gather_upper(True)
    loads[1].wait()
    if head:
        head_gather_low(0, False)
    scatter_rows(cot_v, dout_s, masks)
    for i in range(e):
        gather_round(i, 0)
        if head:
            head_gather_low(i, True)
            if i + 1 < e:
                head_gather_low(i + 1, False)
    unpack(range(near_count))
    if head:
        unpack_head()
    load_matrix(*matrices()[0])
    load_vectors((G1, S1, BQ, BV))
    gvec[...] = jnp.zeros_like(gvec)

    height = x_s.shape[0] // BLOCKS
    bias = jnp.concatenate([param(BQ), jnp.zeros((1, D), F32), param(BV)], axis=1)

    def band(i):
        return pl.ds(pl.multiple_of(i * height, 16), height)

    def project(i, carry):
        hat1, _ = norm_stats(x_s[band(i), :].astype(F32))
        attn_in = (hat1 * param(G1) + param(S1)).astype(BF)
        attn_s[band(i), :] = attn_in
        qkv_s[band(i), :] = (nn(attn_in, wqkv[...]) + bias).astype(BF)
        return carry

    lax.fori_loop(0, BLOCKS, project, 0)

    lane = lax.broadcasted_iota(jnp.int32, (1, LANES), 1)
    low = lane < HD
    low_b = low.astype(BF)
    high_b = 1 - low_b
    key_ok = lax.broadcasted_iota(jnp.int32, (1, tokp), 1) < tok

    def views(t):
        g, p = t // PAIRS, t % PAIRS
        rows = pl.ds(pl.multiple_of(g * tokp, 16), tokp)
        return rows, [pl.ds(pl.multiple_of(j * D + p * LANES, LANES), LANES) for j in range(3)]

    def stack(v, scale=1.0):
        return jnp.concatenate([v * (low_b * scale), v * (high_b * scale)], axis=0)

    def attend(tiles_now):
        at = [views(t) for t in tiles_now]
        q, k, v = ([qkv_s[rows, c[j]] for rows, c in at] for j in range(3))
        s = [jnp.where(key_ok, nt(stack(a, HD**-0.5), b), -1e30) for a, b in zip(q, k)]
        e = [jnp.exp(a - jnp.max(a, axis=-1, keepdims=True)) for a in s]
        probs = [(a * (1.0 / jnp.sum(a, axis=-1, keepdims=True))).astype(BF) for a in e]
        mixed = [nn(a, b) for a, b in zip(probs, v)]
        for t, (rows, c), a, m in zip(tiles_now, at, probs, mixed):
            probs_s[t] = a
            mixed_s[rows, c[0]] = jnp.where(low, m[:tokp], m[tokp:]).astype(BF)

    tiles = slots * PAIRS
    trips = tiles // UNROLL

    def forward(i, carry):
        for r in range(e + 1):
            @pl.when(i == (r * trips) // (e + 1))
            def _():
                if r == 0:
                    for p in range(PARTS):
                        gather_upper_arrive(p, 1)
                else:
                    gather_round(r - 1, 1)

        attend([i * UNROLL + u for u in range(UNROLL)])
        return carry

    lax.fori_loop(0, trips, forward, 0)
    gather_sent()
    unpack(range(near_count, n))
    for m in matrices()[1:]:
        load_matrix(*m)
    load_vectors((BO, G2, S2, BD))
    for c in range(FF // LANES):
        bup[:, c * LANES : (c + 1) * LANES] = buf[3 * ROW_BUP + c : 3 * ROW_BUP + c + 1, :]
    tail = buf.shape[0] - 3 * ROWS
    buf[3 * ROWS :, :] = jnp.zeros((tail, LANES), F32)

    def add_vector(i, value):
        gvec[i : i + 1, :] += value

    def second_norm(i, carry):
        rows = band(i)
        hidden = x_s[rows, :].astype(F32) + nn(mixed_s[rows, :], wout[...]) + param(BO)
        hat2, inv2 = norm_stats(hidden)
        ffn_s[rows, :] = (hat2 * param(G2) + param(S2)).astype(BF)
        hat_s[rows, :] = hat2
        inv_s[rows, :] = inv2
        res_s[rows, :] = hidden + param(BD)
        dn2_s[rows, :] = jnp.zeros((height, D), F32)
        add_vector(BD, colsum(dout_s[rows, :].astype(F32)))
        return carry

    lax.fori_loop(0, BLOCKS, second_norm, 0)

    def feed(c, carry):
        cols = pl.ds(pl.multiple_of(c * CHUNK, CHUNK), CHUNK)
        ffn_in = ffn_s[...]
        dout_b = dout_s[...]
        pre = nn(ffn_in, wup[:, cols]) + bup[:, cols]
        cumul = 0.5 * (1.0 + lax.erf(pre * 0.7071067811865476))
        act = (pre * cumul).astype(BF)
        res_s[...] += nn(act, wdn[cols, :])
        grad = tn(act, dout_b)
        for b in range(3):
            buf[pl.ds(3 * ROW_DOWN + 3 * CHUNK * c + b, CHUNK, 3), :] = grad[
                :, b * LANES : (b + 1) * LANES
            ]
        density = jnp.exp(-0.5 * pre * pre) * 0.3989422804014327
        dpre = nt(dout_b, wdn[cols, :]) * (cumul + pre * density)
        total = colsum(dpre)
        dpre_b = dpre.astype(BF)
        grad = tn(ffn_in, dpre_b)
        for b in range(CHUNK // LANES):
            lanes = slice(b * LANES, (b + 1) * LANES)
            at = c * (CHUNK // LANES) + b
            buf[pl.ds(3 * ROW_UP + at, D, FF // LANES), :] = grad[:, lanes]
            buf[pl.ds(3 * ROW_BUP + at, 1), :] = total[:, lanes]
        dn2_s[...] += nt(dpre_b, wup[:, cols])
        return carry

    lax.fori_loop(0, FF // CHUNK, feed, 0)

    def gather_back(value, source_ref):
        for g in range(slots):
            for c in range(3):
                cols = slice(c * LANES, (c + 1) * LANES)
                v = source_ref[g * tokp : g * tokp + tok, cols]
                if value is not None:
                    v = v * value[g]
                stage[c, pl.ds(g, tok, slots), :] = v

    def emit_rows(target):
        for c in range(3):
            target[:, c * LANES : (c + 1) * LANES] = stage[c].astype(BF)

    def second_norm_back(i, carry):
        rows = band(i)
        hat2 = hat_s[rows, :]
        dn2 = dn2_s[rows, :]
        add_vector(G2, colsum(dn2 * hat2))
        add_vector(S2, colsum(dn2))
        dhidden = dout_s[rows, :].astype(F32) + norm_back(dn2, hat2, inv_s[rows, :], param(G2))
        dn2_s[rows, :] = dhidden
        dhidden_b = dhidden.astype(BF)
        add_vector(BO, colsum(dhidden))
        dout_s[rows, :] = dhidden_b
        ffn_s[rows, :] = nt(dhidden_b, wout[...]).astype(BF)
        return carry

    lax.fori_loop(0, BLOCKS, second_norm_back, 0)
    grad = tn(mixed_s[...], dout_s[...])
    for b in range(3):
        buf[pl.ds(3 * ROW_OUT + b, D, 3), :] = grad[:, b * LANES : (b + 1) * LANES]
    for i in (BO, G2, S2, BD):
        put_vector(i, gvec[i : i + 1, :])
    pack(range(near_count, n))
    for p in range(PARTS):
        reduce_low(p, e - 1, 1).start()
    gather_back(masks, res_s)
    emit_rows(img_v)
    out_copy = pltpu.make_async_copy(img_v, out_ref, load_sem.at[2])
    out_copy.start()

    def attend_back(tiles_now):
        at = [views(t) for t in tiles_now]
        q, k, v = ([qkv_s[rows, c[j]] for rows, c in at] for j in range(3))
        dm = [stack(ffn_s[rows, c[0]]) for rows, c in at]
        probs = [probs_s[t] for t in tiles_now]
        dprobs = [nt(a, b) for a, b in zip(dm, v)]
        dvalue = [tn(a, b) for a, b in zip(probs, dm)]
        wide = [a.astype(F32) for a in probs]
        delta_p = [jnp.sum(a * b, axis=-1, keepdims=True) for a, b in zip(wide, dprobs)]
        ds = [(a * (b - c)).astype(BF) for a, b, c in zip(wide, dprobs, delta_p)]
        dq = [nn(a, b) for a, b in zip(ds, k)]
        dkey = [tn(a, stack(b, HD**-0.5)) for a, b in zip(ds, q)]
        dquery = [jnp.where(low, a[:tokp], a[tokp:]) * (HD**-0.5) for a in dq]
        for (rows, (cq, ck, cv)), a, b, c in zip(at, dquery, dkey, dvalue):
            gvec[BQ : BQ + 1, cq] += colsum(a)
            gvec[BV : BV + 1, cq] += colsum(c)
            qkv_s[rows, cq] = a.astype(BF)
            qkv_s[rows, ck] = b.astype(BF)
            qkv_s[rows, cv] = c.astype(BF)

    def backward(i, carry):
        for r in range(e + 1):
            @pl.when(i == ((r + 1) * trips) // (e + 2))
            def _():
                if r < e:
                    reduce_round(e - 1 - r, 1)
                else:
                    reduce_last(1)

        attend_back([i * UNROLL + u for u in range(UNROLL)])
        return carry

    lax.fori_loop(0, trips, backward, 0)

    def first_norm_back(i, carry):
        rows = band(i)
        dn1 = nt(qkv_s[rows, :], wqkv[...])
        hat1, inv1 = norm_stats(x_s[rows, :].astype(F32))
        add_vector(G1, colsum(dn1 * hat1))
        add_vector(S1, colsum(dn1))
        res_s[rows, :] = dn2_s[rows, :] + norm_back(dn1, hat1, inv1, param(G1))
        return carry

    lax.fori_loop(0, BLOCKS, first_norm_back, 0)

    def grad_qkv(c, carry):
        cols = pl.ds(pl.multiple_of(c * LANES, LANES), LANES)
        grad = tn(attn_s[:, cols], qkv_s[...])
        for b in range(9):
            at = 3 * ROW_QKV + 9 * LANES * c + b
            buf[pl.ds(at, LANES, 9), :] = grad[:, b * LANES : (b + 1) * LANES]
        return carry

    lax.fori_loop(0, 3, grad_qkv, 0)
    for i in (G1, S1, BQ, BV):
        put_vector(i, gvec[i : i + 1, :])
    pack(range(near_count))
    for p in range(PARTS):
        reduce_low(p, e - 1, 0).start()
    if head:
        at = shard * near_count // LANES
        head_v[...] = buf[at : at + 16, :].astype(BF)
    gather_back(None, res_s)
    emit_rows(cot_v)
    din_copy = pltpu.make_async_copy(cot_v, din_ref, load_sem.at[3])
    din_copy.start()
    for i in reversed(range(e)):
        reduce_round(i, 0)
        if head:
            head_reduce_low(i)
    if head:
        head_reduce_upper()
    reduce_last(0)
    reduce_sent()
    out_copy.wait()
    din_copy.wait()


def run_step(n, shard, window, live, mine, images, cotangent):
    tok, slots, _ = images.shape
    tokp = up_to(tok, 16)
    rows = slots * tokp
    flat = (slots * tok, D)
    buf_rows = up_to(max(shard * (n - 1) // LANES + window, 3 * ROWS) + 8, 8)
    whole = pl.BlockSpec(memory_space=pltpu.VMEM)
    apart = pl.BlockSpec(memory_space=pl.ANY)
    VM = pltpu.VMEM
    e, _ = plan(n, shard)
    near_count, uppers = 1 << e, n >> e
    part = window // PARTS
    DMA = pltpu.SemaphoreType.DMA
    across = DMA((PARTS, uppers - 1))
    inside = DMA((2, PARTS, e))
    tops = DMA((uppers - 1 + e,))
    out, din, mine = pl.pallas_call(
        functools.partial(step_kernel, n, shard, slots, tok, tokp),
        in_specs=[pl.BlockSpec(memory_space=pltpu.SMEM), whole, apart, apart],
        out_specs=[apart, apart, whole],
        out_shape=[
            jax.ShapeDtypeStruct(flat, BF),
            jax.ShapeDtypeStruct(flat, BF),
            jax.ShapeDtypeStruct((window, LANES), F32),
        ],
        scratch_shapes=[
            VM((PARTS, near_count, uppers, part, LANES), BF),
            VM((PARTS, near_count - 1, uppers, part, LANES), BF),
            VM((PARTS, uppers - 1, part, LANES), BF),
            VM((16, LANES), BF), VM((e + uppers - 1, 16, LANES), BF),
            VM((buf_rows, LANES), F32),
            VM((D, 3 * D), BF), VM((D, D), BF), VM((D, FF), BF), VM((FF, D), BF),
            VM((8, D), F32), VM((1, FF), F32), VM((8, D), F32),
            VM(flat, BF), VM(flat, BF), VM((3, slots * tok, LANES), F32),
            VM((rows, D), BF), VM((rows, D), BF), VM((rows, D), BF),
            VM((rows, 3 * D), BF), VM((slots * PAIRS, 2 * tokp, tokp), BF),
            VM((rows, D), BF),
            VM((rows, D), F32), VM((rows, 1), F32), VM((rows, D), F32), VM((rows, D), F32), VM((rows, D), BF),
            DMA((4,)), across, across, inside, inside, across, across, inside, inside,
            tops, tops, DMA((1,)), tops,
        ],
        compiler_params=pltpu.CompilerParams(
            collective_id=1, has_side_effects=True, vmem_limit_bytes=67043328
        ),
        name="step",
    )(live, mine, images.reshape(flat), cotangent.reshape(flat))
    return out.reshape(tok, slots, D), din.reshape(tok, slots, D), mine


def shards(params, images, cotangent, live):
    n = lax.axis_size("dp")
    assert n & (n - 1) == 0 and n >= 4
    shard = params.shape[0]
    window = up_to((shard + 2 * LANES - 2) // LANES, 16 * PARTS)
    me = lax.axis_index("dp")
    shift = (shard % LANES) * me % LANES
    padded = jnp.pad(params, (0, window * LANES - shard))
    moved = jnp.roll(padded, shift).astype(BF).reshape(window, LANES)
    images, cotangent = (jnp.transpose(a, (1, 0, 2)) for a in (images, cotangent))
    out, din, mine = run_step(n, shard, window, live, moved, images, cotangent)
    out, din = (jnp.transpose(a, (1, 0, 2)) for a in (out, din))
    flat = lax.dynamic_slice(mine.reshape(-1), (shift,), (shard,))
    return out, din, flat


def solution(mesh):
    return jax.shard_map(
        shards,
        mesh=mesh,
        in_specs=(P("dp"), P("dp", None, None), P("dp", None, None), P("dp")),
        out_specs=(P("dp", None, None), P("dp", None, None), P("dp")),
        check_vma=False,
    )
```

```python
import functools

import jax
import jax.numpy as jnp
from jax import lax
from jax.experimental import pallas as pl
from jax.experimental.pallas import tpu as pltpu
from jax.sharding import PartitionSpec as P

D = 384
HEADS = 6
FF = 1536
HD = D // HEADS
PAIRS = HEADS // 2
EPS = 1e-06
LANES = 128
BF = jnp.bfloat16
F32 = jnp.float32

ROW_QKV = 2
ROW_OUT = 2 + 3 * D + 2
ROW_UP = ROW_OUT + D + 3
ROW_BUP = ROW_UP + FF
ROW_DOWN = ROW_BUP + FF // D
ROW_BDOWN = ROW_DOWN + FF
ROWS = ROW_BDOWN + 1
VEC_ROWS = (0, 1, ROW_OUT - 2, ROW_OUT - 1, ROW_UP - 3, ROW_UP - 2, ROW_UP - 1, ROW_BDOWN)
G1, S1, BQ, BV, BO, G2, S2, BD = range(8)

CHUNK = 512
PARTS = 4
UNROLL = 4
BLOCKS = 4
MESH = pl.DeviceIdType.MESH
HALVES = (range(0, PARTS // 2), range(PARTS // 2, PARTS))


def up_to(value, unit):
    return (value + unit - 1) // unit * unit


def nt(a, b):
    return lax.dot_general(a, b, (((1,), (1,)), ((), ())), preferred_element_type=F32)


def tn(a, b):
    return lax.dot_general(a, b, (((0,), (0,)), ((), ())), preferred_element_type=F32)


def nn(a, b):
    return jnp.dot(a, b, preferred_element_type=F32)


def norm_stats(values):
    center = values - jnp.mean(values, axis=-1, keepdims=True)
    inv = lax.rsqrt(jnp.mean(center * center, axis=-1, keepdims=True) + EPS)
    return center * inv, inv


def norm_back(grad_out, hat, inv, gain):
    g = grad_out * gain
    return inv * (
        g
        - jnp.mean(g, axis=-1, keepdims=True)
        - hat * jnp.mean(g * hat, axis=-1, keepdims=True)
    )


def colsum(v):
    return jnp.sum(v, axis=0, keepdims=True)


def low_orders(low_bits):
    near = list(range(low_bits))[::-1]
    swapped = near[1:2] + near[:1] + near[2:] if low_bits > 2 else near
    return [near, swapped] * (PARTS // 2)


def place(low, order):
    return sum((low >> b & 1) << i for i, b in enumerate(order))


def reduce_waves(uppers):
    return [(0, 1), (1, 2)] + ([(2, uppers)] if uppers > 2 else [])


def plan(n, shard):
    needed = -(-3 * ROW_OUT * LANES // shard)
    low_bits = max(needed.bit_length() - 1, 1)
    if needed > (1 << low_bits) + 1:
        low_bits += 1
    low_bits = min(low_bits, n.bit_length() - 2)
    head = 3 * ROW_OUT - (shard << low_bits) // LANES
    assert head <= 16
    return low_bits, max(head, 0)


def matrices():
    return (
        (0, D, 9, ROW_QKV),
        (1, D, 3, ROW_OUT),
        (2, D, 12, ROW_UP),
        (3, FF, 3, ROW_DOWN),
    )


def step_kernel(
    n, shard, slots, tok, tokp,
    live_ref, mine_ref, img_hbm, cot_hbm,
    out_ref, din_ref, flat_ref,
    gath, recv, recv_up, head_v, head_in, buf, wqkv, wout, wup, wdn, vec, bup, gvec,
    img_v, cot_v, stage, x_s, dout_s, attn_s, qkv_s, probs_s, mixed_s,
    hat_s, inv_s, res_s, dn2_s, ffn_s,
    load_sem, gu_send, gu_recv, gl_send, gl_recv,
    ru_send, ru_recv, rl_send, rl_recv, gh_send, gh_recv, rh_send, rh_recv,
):
    bits = n.bit_length() - 1
    me = lax.axis_index("dp")
    window = mine_ref.shape[0]
    part = window // PARTS
    weights = (wqkv, wout, wup, wdn)
    delta = [(1 - 2 * (me // (1 << b) % 2)) * (1 << b) for b in range(bits)]
    bit = [me // (1 << b) % 2 for b in range(bits)]
    e, head = plan(n, shard)
    near_count, uppers = 1 << e, n >> e
    up = me // near_count
    near_me = me % near_count
    orders = low_orders(e)
    spots = [sum(bit[b] * (1 << i) for i, b in enumerate(order)) for order in orders]
    waves = (pl.ds(0, 1), pl.ds(1, uppers - 1))
    r_waves = reduce_waves(uppers)

    def peer(j):
        return me + sum(delta[e + b] for b in range(bits - e) if j >> b & 1)

    def fixed(p, i):
        return sum(bit[b] * (1 << k) for k, b in enumerate(orders[p]) if k >= i)

    def remote(src, dst, send, recv_at, to):
        return pltpu.make_async_remote_copy(
            src_ref=src, dst_ref=dst, send_sem=send, recv_sem=recv_at,
            device_id=(to,), device_id_type=MESH,
        )

    def gather_upper(p, j):
        return remote(
            mine_ref.at[pl.ds(p * part, part)], gath.at[p, spots[p], up],
            gu_send.at[p, j - 1], gu_recv.at[p, j - 1], peer(j),
        )

    def gather_low(p, i, wave):
        held = gath.at[p, pl.ds(fixed(p, i), 1 << i), waves[wave]]
        return remote(
            held, held, gl_send.at[wave, p, i], gl_recv.at[wave, p, i],
            me + delta[orders[p][i]],
        )

    def send_own():
        for p in range(PARTS):
            for j in range(1, uppers):
                gather_upper(p, j).start()

    def gather_upper_arrive(p, wave):
        own = gath.at[p, spots[p], up]
        if wave == 0:
            @pl.when(up > 0)
            def _():
                remote(own, own, gu_send.at[p, 0], gu_recv.at[p, up - 1], me).wait_recv()
        else:
            for j in range(1, uppers):
                @pl.when(up != j)
                def _():
                    remote(own, own, gu_send.at[p, 0], gu_recv.at[p, j - 1], me).wait_recv()
        gather_low(p, 0, wave).start()

    def gather_round(i, wave, parts=range(PARTS)):
        for p in parts:
            gather_low(p, i, wave).wait_recv()
            if i + 1 < e:
                gather_low(p, i + 1, wave).start()

    def zero_from(i):
        return sum(bit[b] for b in orders[0][i:]) if i < e else 0

    def head_gather_upper(wait):
        if wait:
            @pl.when(zero_from(0) + (up == 1).astype(jnp.int32) == 0)
            def _():
                at = up + 1 - 2 * (up % 2) - 1
                remote(head_v, head_v, gh_send.at[0], gh_recv.at[at], me).wait_recv()
        else:
            @pl.when(me == near_count)
            def _():
                head_v[...] = mine_ref[0:16, :]
                for j in range(1, uppers):
                    remote(
                        mine_ref.at[0:16], head_v, gh_send.at[j - 1], gh_recv.at[j - 1], peer(j)
                    ).start()

    def head_gather_low(i, wait):
        at = uppers - 1 + i
        copy = remote(head_v, head_v, gh_send.at[at], gh_recv.at[at], me + delta[orders[0][i]])
        if wait:
            @pl.when(zero_from(i + 1) * 2 + bit[orders[0][i]] == 1)
            def _():
                copy.wait_recv()
        else:
            @pl.when(zero_from(i) == 0)
            def _():
                copy.start()

    def gather_sent():
        for p in range(PARTS):
            for j in range(1, uppers):
                gather_upper(p, j).wait_send()
            for i in range(e):
                for wave in range(2):
                    gather_low(p, i, wave).wait_send()
        if head:
            @pl.when(me == near_count)
            def _():
                for j in range(1, uppers):
                    remote(
                        mine_ref.at[0:16], head_v, gh_send.at[j - 1], gh_recv.at[j - 1], peer(j)
                    ).wait_send()
            for i in range(e):
                @pl.when(zero_from(i) == 0)
                def _():
                    at = uppers - 1 + i
                    remote(
                        head_v, head_v, gh_send.at[at], gh_recv.at[at], me + delta[orders[0][i]]
                    ).wait_send()

    def span(wave):
        first, last = r_waves[wave]
        return pl.ds(first, last - first)

    def reduce_low(p, i, wave):
        other = fixed(p, i + 1) + (1 - bit[orders[p][i]]) * (1 << i)
        return remote(
            gath.at[p, pl.ds(other, 1 << i), span(wave)],
            recv.at[p, pl.ds((1 << i) - 1, 1 << i), span(wave)],
            rl_send.at[wave, p, i], rl_recv.at[wave, p, i], me + delta[orders[p][i]],
        )

    def reduce_upper(p, j, block, to):
        return remote(
            gath.at[p, spots[p], block], recv_up.at[p, j - 1],
            ru_send.at[p, j - 1], ru_recv.at[p, j - 1], to,
        )

    def reduce_upper_start(p, wave):
        first, last = r_waves[wave]
        for j in range(1, uppers):
            to = peer(j) // near_count

            @pl.when((to >= first) & (to < last))
            def _():
                reduce_upper(p, j, to, peer(j)).start()

    def reduce_round(i, wave):
        for p in range(PARTS):
            reduce_low(p, i, wave).wait_recv()
            keep = pl.ds(fixed(p, i), 1 << i)
            slot = pl.ds((1 << i) - 1, 1 << i)
            total = gath[p, keep, span(wave)].astype(F32) + recv[p, slot, span(wave)].astype(F32)
            gath[p, keep, span(wave)] = total.astype(BF)
            if i > 0:
                reduce_low(p, i - 1, wave).start()
            else:
                reduce_upper_start(p, wave)

    def reduce_last(wave):
        @pl.when(up == 0 if wave == 0 else up > 0)
        def _():
            for p in range(PARTS):
                total = gath[p, spots[p], up].astype(F32)
                for j in range(1, uppers):
                    reduce_upper(p, j, 0, me).wait_recv()
                    total = total + recv_up[p, j - 1].astype(F32)
                flat_ref[p * part : (p + 1) * part, :] = total

    def head_reduce_low(i):
        copy = remote(
            head_v, head_in.at[i], rh_send.at[0], rh_recv.at[i], me + delta[orders[0][i]]
        )

        @pl.when(zero_from(i + 1) * 2 + bit[orders[0][i]] == 1)
        def _():
            copy.start()
            copy.wait_send()

        @pl.when(zero_from(i) == 0)
        def _():
            copy.wait_recv()
            head_v[...] = (head_v[...].astype(F32) + head_in[i].astype(F32)).astype(BF)

    def head_reduce_upper():
        @pl.when(zero_from(0) + (up == 1).astype(jnp.int32) == 0)
        def _():
            at = up + 1 - 2 * (up % 2) - 1
            copy = remote(head_v, head_in.at[e + at], rh_send.at[0], rh_recv.at[e + at], near_count)
            copy.start()
            copy.wait_send()

    def head_reduce_last():
        @pl.when(me == near_count)
        def _():
            total = head_v[...].astype(F32)
            for j in range(1, uppers):
                at = e + j - 1
                remote(head_v, head_in.at[at], rh_send.at[0], rh_recv.at[at], me).wait_recv()
                total = total + head_in[at].astype(F32)
            flat_ref[0:16, :] = total

    def reduce_sent():
        for p in range(PARTS):
            for j in range(1, uppers):
                reduce_upper(p, j, 0, me).wait_send()
            for i in range(e):
                for wave in range(len(r_waves)):
                    reduce_low(p, i, wave).wait_send()

    def home(d, p):
        return p, place(d % near_count, orders[p]), d // near_count

    def unpack(blocks):
        for d in blocks:
            first, shift = divmod(shard * d, LANES)
            rows = (shift + shard + LANES - 1) // LANES
            for p in range(PARTS):
                count = min(part, rows - p * part)
                if count <= 0:
                    break
                at = first + p * part
                piece = gath[home(d, p)].astype(F32)
                if d > 0 and shift and p == 0:
                    seam = buf[at : at + 1, :] + piece[0:1]
                    buf[at : at + count, :] = piece[:count]
                    buf[at : at + 1, :] = seam
                else:
                    buf[at : at + count, :] = piece[:count]

    def unpack_head():
        first, shift = divmod(shard * near_count, LANES)
        piece = head_v[...].astype(F32)
        if shift:
            piece = piece + jnp.where(
                lax.broadcasted_iota(jnp.int32, piece.shape, 0) == 0, buf[first : first + 16, :], 0.0
            )
        buf[first : first + 16, :] = piece

    def load_matrix(k, rows, blocks, start):
        for b in range(blocks):
            weights[k][:, b * LANES : (b + 1) * LANES] = buf[
                pl.ds(3 * start + b, rows, blocks), :
            ].astype(BF)

    def load_vectors(indices):
        for i in indices:
            r = VEC_ROWS[i]
            for c in range(3):
                vec[i : i + 1, c * LANES : (c + 1) * LANES] = buf[3 * r + c : 3 * r + c + 1, :]

    def put_vector(i, value):
        r = VEC_ROWS[i]
        for c in range(3):
            buf[3 * r + c : 3 * r + c + 1, :] = value[:, c * LANES : (c + 1) * LANES]

    def pack(blocks):
        for d in blocks:
            first = shard * d // LANES
            for p in range(PARTS):
                at = first + p * part
                gath[home(d, p)] = buf[at : at + part, :].astype(BF)

    def param(i):
        return vec[i : i + 1, :]

    loads = [
        pltpu.make_async_copy(img_hbm, img_v, load_sem.at[0]),
        pltpu.make_async_copy(cot_hbm, cot_v, load_sem.at[1]),
    ]
    for c in loads:
        c.start()
    partners = [me + delta[b] for b in range(e)] + [peer(j) for j in range(1, uppers)]
    barrier = pltpu.get_barrier_semaphore()
    for partner in partners:
        pl.semaphore_signal(barrier, inc=1, device_id=(partner,), device_id_type=MESH)
    pl.semaphore_wait(barrier, len(partners))

    @pl.when(up == 0)
    def _():
        send_own()

    if head:
        head_gather_upper(False)
    for p in range(PARTS):
        gath[p, spots[p], up] = mine_ref[p * part : (p + 1) * part, :]

    def scatter_rows(source, target, scales):
        for c in range(3):
            stage[c] = source[:, c * LANES : (c + 1) * LANES].astype(F32)
        target[...] = jnp.zeros_like(target)
        for g in range(slots):
            for c in range(3):
                cols = slice(c * LANES, (c + 1) * LANES)
                v = stage[c, pl.ds(g, tok, slots), :]
                if scales is not None:
                    v = v * scales[g]
                target[g * tokp : g * tokp + tok, cols] = v.astype(BF)

    live = live_ref[0]
    masks = [(g < live).astype(F32) for g in range(slots)]
    loads[0].wait()
    scatter_rows(img_v, x_s, None)
    for p in range(PARTS):
        gather_upper_arrive(p, 0)

    @pl.when(up > 0)
    def _():
        send_own()

    if head:
        head_gather_upper(True)
    loads[1].wait()
    if head:
        head_gather_low(0, False)
    scatter_rows(cot_v, dout_s, masks)
    for i in range(e):
        gather_round(i, 0)
        if head:
            head_gather_low(i, True)
            if i + 1 < e:
                head_gather_low(i + 1, False)
    for p in range(PARTS):
        gather_upper_arrive(p, 1)
    unpack(range(near_count))
    if head:
        unpack_head()
    load_matrix(*matrices()[0])
    load_vectors((G1, S1, BQ, BV))
    gvec[...] = jnp.zeros_like(gvec)

    height = x_s.shape[0] // BLOCKS
    bias = jnp.concatenate([param(BQ), jnp.zeros((1, D), F32), param(BV)], axis=1)

    def band(i):
        return pl.ds(pl.multiple_of(i * height, 16), height)

    def project(i, carry):
        for half in range(2):
            @pl.when(i == 1 + half * (BLOCKS - 2))
            def _():
                gather_round(0, 1, HALVES[half])

        hat1, _ = norm_stats(x_s[band(i), :].astype(F32))
        attn_in = (hat1 * param(G1) + param(S1)).astype(BF)
        attn_s[band(i), :] = attn_in
        qkv_s[band(i), :] = (nn(attn_in, wqkv[...]) + bias).astype(BF)
        return carry

    lax.fori_loop(0, BLOCKS, project, 0)

    lane = lax.broadcasted_iota(jnp.int32, (1, LANES), 1)
    low = lane < HD
    low_b = low.astype(BF)
    high_b = 1 - low_b
    key_ok = lax.broadcasted_iota(jnp.int32, (1, tokp), 1) < tok

    def views(t):
        g, p = t // PAIRS, t % PAIRS
        rows = pl.ds(pl.multiple_of(g * tokp, 16), tokp)
        return rows, [pl.ds(pl.multiple_of(j * D + p * LANES, LANES), LANES) for j in range(3)]

    def stack(v, scale=1.0):
        return jnp.concatenate([v * (low_b * scale), v * (high_b * scale)], axis=0)

    def attend(tiles_now):
        at = [views(t) for t in tiles_now]
        q, k, v = ([qkv_s[rows, c[j]] for rows, c in at] for j in range(3))
        s = [jnp.where(key_ok, nt(stack(a, HD**-0.5), b), -1e30) for a, b in zip(q, k)]
        e = [jnp.exp(a - jnp.max(a, axis=-1, keepdims=True)) for a in s]
        probs = [(a * (1.0 / jnp.sum(a, axis=-1, keepdims=True))).astype(BF) for a in e]
        mixed = [nn(a, b) for a, b in zip(probs, v)]
        for t, (rows, c), a, m in zip(tiles_now, at, probs, mixed):
            probs_s[t] = a
            mixed_s[rows, c[0]] = jnp.where(low, m[:tokp], m[tokp:]).astype(BF)

    tiles = slots * PAIRS
    trips = tiles // UNROLL

    def forward(i, carry):
        for r in range(1, e - 1):
            for half in range(2):
                @pl.when(i == (trips * (2 * r + half) - 1) // (2 * e - 3))
                def _():
                    gather_round(r, 1, HALVES[half])

        attend([i * UNROLL + u for u in range(UNROLL)])
        return carry

    lax.fori_loop(0, trips, forward, 0)
    gather_round(e - 1, 1)
    gather_sent()
    unpack(range(near_count, n))
    for m in matrices()[1:]:
        load_matrix(*m)
    load_vectors((BO, G2, S2, BD))
    for c in range(FF // LANES):
        bup[:, c * LANES : (c + 1) * LANES] = buf[3 * ROW_BUP + c : 3 * ROW_BUP + c + 1, :]
    tail = buf.shape[0] - 3 * ROWS
    buf[3 * ROWS :, :] = jnp.zeros((tail, LANES), F32)

    def add_vector(i, value):
        gvec[i : i + 1, :] += value

    def second_norm(i, carry):
        rows = band(i)
        hidden = x_s[rows, :].astype(F32) + nn(mixed_s[rows, :], wout[...]) + param(BO)
        hat2, inv2 = norm_stats(hidden)
        ffn_s[rows, :] = (hat2 * param(G2) + param(S2)).astype(BF)
        hat_s[rows, :] = hat2
        inv_s[rows, :] = inv2
        res_s[rows, :] = hidden + param(BD)
        dn2_s[rows, :] = jnp.zeros((height, D), F32)
        add_vector(BD, colsum(dout_s[rows, :].astype(F32)))
        return carry

    lax.fori_loop(0, BLOCKS, second_norm, 0)
    put_vector(BD, gvec[BD : BD + 1, :])

    def feed(c, carry):
        cols = pl.ds(pl.multiple_of(c * CHUNK, CHUNK), CHUNK)
        ffn_in = ffn_s[...]
        dout_b = dout_s[...]
        pre = nn(ffn_in, wup[:, cols]) + bup[:, cols]
        cumul = 0.5 * (1.0 + lax.erf(pre * 0.7071067811865476))
        act = (pre * cumul).astype(BF)
        res_s[...] += nn(act, wdn[cols, :])
        grad = tn(act, dout_b)
        for b in range(3):
            buf[pl.ds(3 * ROW_DOWN + 3 * CHUNK * c + b, CHUNK, 3), :] = grad[
                :, b * LANES : (b + 1) * LANES
            ]
        density = jnp.exp(-0.5 * pre * pre) * 0.3989422804014327
        dpre = nt(dout_b, wdn[cols, :]) * (cumul + pre * density)
        total = colsum(dpre)
        dpre_b = dpre.astype(BF)
        grad = tn(ffn_in, dpre_b)
        for b in range(CHUNK // LANES):
            lanes = slice(b * LANES, (b + 1) * LANES)
            at = c * (CHUNK // LANES) + b
            buf[pl.ds(3 * ROW_UP + at, D, FF // LANES), :] = grad[:, lanes]
            buf[pl.ds(3 * ROW_BUP + at, 1), :] = total[:, lanes]
        dn2_s[...] += nt(dpre_b, wup[:, cols])
        return carry

    lax.fori_loop(0, FF // CHUNK, feed, 0)
    assert shard * 2 * near_count // LANES >= 3 * ROW_UP

    def send_blocks(wave):
        first, last = r_waves[wave]
        pack(range(first * near_count, last * near_count))
        for p in range(PARTS):
            reduce_low(p, e - 1, wave).start()

    for wave in range(2, len(r_waves)):
        send_blocks(wave)

    def gather_back(value, source_ref):
        for g in range(slots):
            for c in range(3):
                cols = slice(c * LANES, (c + 1) * LANES)
                v = source_ref[g * tokp : g * tokp + tok, cols]
                if value is not None:
                    v = v * value[g]
                stage[c, pl.ds(g, tok, slots), :] = v

    def emit_rows(target):
        for c in range(3):
            target[:, c * LANES : (c + 1) * LANES] = stage[c].astype(BF)

    def second_norm_back(i, carry):
        rows = band(i)
        hat2 = hat_s[rows, :]
        dn2 = dn2_s[rows, :]
        add_vector(G2, colsum(dn2 * hat2))
        add_vector(S2, colsum(dn2))
        dhidden = dout_s[rows, :].astype(F32) + norm_back(dn2, hat2, inv_s[rows, :], param(G2))
        dn2_s[rows, :] = dhidden
        dhidden_b = dhidden.astype(BF)
        add_vector(BO, colsum(dhidden))
        dout_s[rows, :] = dhidden_b
        ffn_s[rows, :] = nt(dhidden_b, wout[...]).astype(BF)
        return carry

    lax.fori_loop(0, BLOCKS, second_norm_back, 0)
    grad = tn(mixed_s[...], dout_s[...])
    for b in range(3):
        buf[pl.ds(3 * ROW_OUT + b, D, 3), :] = grad[:, b * LANES : (b + 1) * LANES]
    for i in (BO, G2, S2):
        put_vector(i, gvec[i : i + 1, :])
    send_blocks(1)
    gather_back(masks, res_s)
    emit_rows(img_v)
    out_copy = pltpu.make_async_copy(img_v, out_ref, load_sem.at[2])
    out_copy.start()

    def attend_back(tiles_now):
        at = [views(t) for t in tiles_now]
        q, k, v = ([qkv_s[rows, c[j]] for rows, c in at] for j in range(3))
        dm = [stack(ffn_s[rows, c[0]]) for rows, c in at]
        probs = [probs_s[t] for t in tiles_now]
        dprobs = [nt(a, b) for a, b in zip(dm, v)]
        dvalue = [tn(a, b) for a, b in zip(probs, dm)]
        wide = [a.astype(F32) for a in probs]
        delta_p = [jnp.sum(a * b, axis=-1, keepdims=True) for a, b in zip(wide, dprobs)]
        ds = [(a * (b - c)).astype(BF) for a, b, c in zip(wide, dprobs, delta_p)]
        dq = [nn(a, b) for a, b in zip(ds, k)]
        dkey = [tn(a, stack(b, HD**-0.5)) for a, b in zip(ds, q)]
        dquery = [jnp.where(low, a[:tokp], a[tokp:]) * (HD**-0.5) for a in dq]
        for (rows, (cq, ck, cv)), a, b, c in zip(at, dquery, dkey, dvalue):
            gvec[BQ : BQ + 1, cq] += colsum(a)
            gvec[BV : BV + 1, cq] += colsum(c)
            qkv_s[rows, cq] = a.astype(BF)
            qkv_s[rows, ck] = b.astype(BF)
            qkv_s[rows, cv] = c.astype(BF)

    def backward(i, carry):
        late = list(range(len(r_waves) - 1, 0, -1))
        points = (e - 1) * len(late)
        for k in range(points):
            @pl.when(i == 1 + (k * (trips - 1)) // points)
            def _():
                reduce_round(e - 1 - k // len(late), late[k % len(late)])

        attend_back([i * UNROLL + u for u in range(UNROLL)])
        return carry

    lax.fori_loop(0, trips, backward, 0)

    def first_norm_back(i, carry):
        for k in range(1, len(r_waves)):
            @pl.when(i == 2 * (len(r_waves) - k) - 1)
            def _():
                reduce_round(0, k)

        rows = band(i)
        dn1 = nt(qkv_s[rows, :], wqkv[...])
        hat1, inv1 = norm_stats(x_s[rows, :].astype(F32))
        add_vector(G1, colsum(dn1 * hat1))
        add_vector(S1, colsum(dn1))
        res_s[rows, :] = dn2_s[rows, :] + norm_back(dn1, hat1, inv1, param(G1))
        return carry

    lax.fori_loop(0, BLOCKS, first_norm_back, 0)

    def grad_qkv(c, carry):
        cols = pl.ds(pl.multiple_of(c * LANES, LANES), LANES)
        grad = tn(attn_s[:, cols], qkv_s[...])
        for b in range(9):
            at = 3 * ROW_QKV + 9 * LANES * c + b
            buf[pl.ds(at, LANES, 9), :] = grad[:, b * LANES : (b + 1) * LANES]
        return carry

    lax.fori_loop(0, 3, grad_qkv, 0)
    for i in (G1, S1, BQ, BV):
        put_vector(i, gvec[i : i + 1, :])
    send_blocks(0)
    if head:
        at = shard * near_count // LANES
        head_v[...] = buf[at : at + 16, :].astype(BF)
    gather_back(None, res_s)
    emit_rows(cot_v)
    din_copy = pltpu.make_async_copy(cot_v, din_ref, load_sem.at[3])
    din_copy.start()
    for i in reversed(range(e)):
        reduce_round(i, 0)
        if head:
            head_reduce_low(i)
    if head:
        head_reduce_upper()
    reduce_last(1)
    reduce_last(0)
    if head:
        head_reduce_last()
    reduce_sent()
    out_copy.wait()
    din_copy.wait()


def run_step(n, shard, window, live, mine, images, cotangent):
    tok, slots, _ = images.shape
    tokp = up_to(tok, 16)
    rows = slots * tokp
    flat = (slots * tok, D)
    buf_rows = up_to(max(shard * (n - 1) // LANES + window, 3 * ROWS) + 8, 8)
    whole = pl.BlockSpec(memory_space=pltpu.VMEM)
    apart = pl.BlockSpec(memory_space=pl.ANY)
    VM = pltpu.VMEM
    e, _ = plan(n, shard)
    near_count, uppers = 1 << e, n >> e
    part = window // PARTS
    DMA = pltpu.SemaphoreType.DMA
    across = DMA((PARTS, uppers - 1))
    inside = DMA((2, PARTS, e))
    summed = DMA((len(reduce_waves(uppers)), PARTS, e))
    tops = DMA((uppers - 1 + e,))
    out, din, mine = pl.pallas_call(
        functools.partial(step_kernel, n, shard, slots, tok, tokp),
        in_specs=[pl.BlockSpec(memory_space=pltpu.SMEM), whole, apart, apart],
        out_specs=[apart, apart, whole],
        out_shape=[
            jax.ShapeDtypeStruct(flat, BF),
            jax.ShapeDtypeStruct(flat, BF),
            jax.ShapeDtypeStruct((window, LANES), F32),
        ],
        scratch_shapes=[
            VM((PARTS, near_count, uppers, part, LANES), BF),
            VM((PARTS, near_count - 1, uppers, part, LANES), BF),
            VM((PARTS, uppers - 1, part, LANES), BF),
            VM((16, LANES), BF), VM((e + uppers - 1, 16, LANES), BF),
            VM((buf_rows, LANES), F32),
            VM((D, 3 * D), BF), VM((D, D), BF), VM((D, FF), BF), VM((FF, D), BF),
            VM((8, D), F32), VM((1, FF), F32), VM((8, D), F32),
            VM(flat, BF), VM(flat, BF), VM((3, slots * tok, LANES), F32),
            VM((rows, D), BF), VM((rows, D), BF), VM((rows, D), BF),
            VM((rows, 3 * D), BF), VM((slots * PAIRS, 2 * tokp, tokp), BF),
            VM((rows, D), BF),
            VM((rows, D), F32), VM((rows, 1), F32), VM((rows, D), F32), VM((rows, D), F32), VM((rows, D), BF),
            DMA((4,)), across, across, inside, inside, across, across, summed, summed,
            tops, tops, DMA((1,)), tops,
        ],
        compiler_params=pltpu.CompilerParams(
            collective_id=1, has_side_effects=True, vmem_limit_bytes=67043328
        ),
        name="step",
    )(live, mine, images.reshape(flat), cotangent.reshape(flat))
    return out.reshape(tok, slots, D), din.reshape(tok, slots, D), mine


def shards(params, images, cotangent, live):
    n = lax.axis_size("dp")
    assert n & (n - 1) == 0 and n >= 4
    shard = params.shape[0]
    window = up_to((shard + 2 * LANES - 2) // LANES, 16 * PARTS)
    me = lax.axis_index("dp")
    shift = (shard % LANES) * me % LANES
    padded = jnp.pad(params, (0, window * LANES - shard))
    moved = jnp.roll(padded, shift).astype(BF).reshape(window, LANES)
    images, cotangent = (jnp.transpose(a, (1, 0, 2)) for a in (images, cotangent))
    out, din, mine = run_step(n, shard, window, live, moved, images, cotangent)
    out, din = (jnp.transpose(a, (1, 0, 2)) for a in (out, din))
    flat = lax.dynamic_slice(mine.reshape(-1), (shift,), (shard,))
    return out, din, flat


def solution(mesh):
    return jax.shard_map(
        shards,
        mesh=mesh,
        in_specs=(P("dp"), P("dp", None, None), P("dp", None, None), P("dp")),
        out_specs=(P("dp", None, None), P("dp", None, None), P("dp")),
        check_vma=False,
    )
```

```python
import functools

import jax
import jax.numpy as jnp
from jax import lax
from jax.experimental import pallas as pl
from jax.experimental.pallas import tpu as pltpu
from jax.sharding import PartitionSpec as P

D = 384
HEADS = 6
FF = 1536
HD = D // HEADS
PAIRS = HEADS // 2
EPS = 1e-06
LANES = 128
BF = jnp.bfloat16
F32 = jnp.float32

ROW_QKV = 2
ROW_OUT = 2 + 3 * D + 2
ROW_UP = ROW_OUT + D + 3
ROW_BUP = ROW_UP + FF
ROW_DOWN = ROW_BUP + FF // D
ROW_BDOWN = ROW_DOWN + FF
ROWS = ROW_BDOWN + 1
VEC_ROWS = (0, 1, ROW_OUT - 2, ROW_OUT - 1, ROW_UP - 3, ROW_UP - 2, ROW_UP - 1, ROW_BDOWN)
G1, S1, BQ, BV, BO, G2, S2, BD = range(8)

CHUNK = 512
PARTS = 4
UNROLL = 4
BLOCKS = 4
MESH = pl.DeviceIdType.MESH
HALVES = (range(0, PARTS // 2), range(PARTS // 2, PARTS))


def up_to(value, unit):
    return (value + unit - 1) // unit * unit


def nt(a, b):
    return lax.dot_general(a, b, (((1,), (1,)), ((), ())), preferred_element_type=F32)


def tn(a, b):
    return lax.dot_general(a, b, (((0,), (0,)), ((), ())), preferred_element_type=F32)


def nn(a, b):
    return jnp.dot(a, b, preferred_element_type=F32)


def norm_stats(values):
    center = values - jnp.mean(values, axis=-1, keepdims=True)
    inv = lax.rsqrt(jnp.mean(center * center, axis=-1, keepdims=True) + EPS)
    return center * inv, inv


def norm_back(grad_out, hat, inv, gain):
    g = grad_out * gain
    return inv * (
        g
        - jnp.mean(g, axis=-1, keepdims=True)
        - hat * jnp.mean(g * hat, axis=-1, keepdims=True)
    )


def colsum(v):
    return jnp.sum(v, axis=0, keepdims=True)


def low_orders(low_bits):
    near = list(range(low_bits))[::-1]
    swapped = near[1:2] + near[:1] + near[2:] if low_bits > 2 else near
    return [near, swapped] * (PARTS // 2)


def place(low, order):
    return sum((low >> b & 1) << i for i, b in enumerate(order))


def reduce_waves(uppers):
    return [(0, 1), (1, 2)] + ([(2, uppers)] if uppers > 2 else [])


def plan(n, shard):
    needed = -(-3 * ROW_OUT * LANES // shard)
    low_bits = max(needed.bit_length() - 1, 1)
    if needed > (1 << low_bits) + 1:
        low_bits += 1
    low_bits = min(low_bits, n.bit_length() - 2)
    head = 3 * ROW_OUT - (shard << low_bits) // LANES
    assert head <= 16
    return low_bits, max(head, 0)


def matrices():
    return (
        (0, D, 9, ROW_QKV),
        (1, D, 3, ROW_OUT),
        (2, D, 12, ROW_UP),
        (3, FF, 3, ROW_DOWN),
    )


def step_kernel(
    n, shard, slots, tok, tokp,
    live_ref, mine_ref, img_hbm, cot_hbm,
    out_ref, din_ref, flat_ref,
    gath, recv, recv_up, head_v, head_in, buf, wqkv, wout, wup, wdn, vec, bup, gvec,
    img_v, cot_v, stage, x_s, dout_s, attn_s, qkv_s, probs_s, mixed_s,
    hat_s, inv_s, res_s, dn2_s, ffn_s,
    load_sem, gu_send, gu_recv, gl_send, gl_recv,
    ru_send, ru_recv, rl_send, rl_recv, gh_send, gh_recv, rh_send, rh_recv,
):
    bits = n.bit_length() - 1
    me = lax.axis_index("dp")
    window = mine_ref.shape[0]
    part = window // PARTS
    weights = (wqkv, wout, wup, wdn)
    delta = [(1 - 2 * (me // (1 << b) % 2)) * (1 << b) for b in range(bits)]
    bit = [me // (1 << b) % 2 for b in range(bits)]
    e, head = plan(n, shard)
    near_count, uppers = 1 << e, n >> e
    up = me // near_count
    near_me = me % near_count
    orders = low_orders(e)
    spots = [sum(bit[b] * (1 << i) for i, b in enumerate(order)) for order in orders]
    waves = (pl.ds(0, 1), pl.ds(1, uppers - 1))
    r_waves = reduce_waves(uppers)

    def peer(j):
        return me + sum(delta[e + b] for b in range(bits - e) if j >> b & 1)

    def fixed(p, i):
        return sum(bit[b] * (1 << k) for k, b in enumerate(orders[p]) if k >= i)

    def remote(src, dst, send, recv_at, to):
        return pltpu.make_async_remote_copy(
            src_ref=src, dst_ref=dst, send_sem=send, recv_sem=recv_at,
            device_id=(to,), device_id_type=MESH,
        )

    def gather_upper(p, j):
        return remote(
            mine_ref.at[pl.ds(p * part, part)], gath.at[p, spots[p], up],
            gu_send.at[p, j - 1], gu_recv.at[p, j - 1], peer(j),
        )

    def gather_low(p, i, wave):
        held = gath.at[p, pl.ds(fixed(p, i), 1 << i), waves[wave]]
        return remote(
            held, held, gl_send.at[wave, p, i], gl_recv.at[wave, p, i],
            me + delta[orders[p][i]],
        )

    def send_own():
        for p in range(PARTS):
            for j in range(1, uppers):
                gather_upper(p, j).start()

    def gather_upper_arrive(p, wave):
        own = gath.at[p, spots[p], up]
        if wave == 0:
            @pl.when(up > 0)
            def _():
                remote(own, own, gu_send.at[p, 0], gu_recv.at[p, up - 1], me).wait_recv()
        else:
            for j in range(1, uppers):
                @pl.when(up != j)
                def _():
                    remote(own, own, gu_send.at[p, 0], gu_recv.at[p, j - 1], me).wait_recv()
        gather_low(p, 0, wave).start()

    def gather_round(i, wave, parts=range(PARTS)):
        for p in parts:
            gather_low(p, i, wave).wait_recv()
            if i + 1 < e:
                gather_low(p, i + 1, wave).start()

    def zero_from(i):
        return sum(bit[b] for b in orders[0][i:]) if i < e else 0

    def head_gather_upper(wait):
        if wait:
            @pl.when(zero_from(0) + (up == 1).astype(jnp.int32) == 0)
            def _():
                at = up + 1 - 2 * (up % 2) - 1
                remote(head_v, head_v, gh_send.at[0], gh_recv.at[at], me).wait_recv()
        else:
            @pl.when(me == near_count)
            def _():
                head_v[...] = mine_ref[0:16, :]
                for j in range(1, uppers):
                    remote(
                        mine_ref.at[0:16], head_v, gh_send.at[j - 1], gh_recv.at[j - 1], peer(j)
                    ).start()

    def head_gather_low(i, wait):
        at = uppers - 1 + i
        copy = remote(head_v, head_v, gh_send.at[at], gh_recv.at[at], me + delta[orders[0][i]])
        if wait:
            @pl.when(zero_from(i + 1) * 2 + bit[orders[0][i]] == 1)
            def _():
                copy.wait_recv()
        else:
            @pl.when(zero_from(i) == 0)
            def _():
                copy.start()

    def gather_sent():
        for p in range(PARTS):
            for j in range(1, uppers):
                gather_upper(p, j).wait_send()
            for i in range(e):
                for wave in range(2):
                    gather_low(p, i, wave).wait_send()
        if head:
            @pl.when(me == near_count)
            def _():
                for j in range(1, uppers):
                    remote(
                        mine_ref.at[0:16], head_v, gh_send.at[j - 1], gh_recv.at[j - 1], peer(j)
                    ).wait_send()
            for i in range(e):
                @pl.when(zero_from(i) == 0)
                def _():
                    at = uppers - 1 + i
                    remote(
                        head_v, head_v, gh_send.at[at], gh_recv.at[at], me + delta[orders[0][i]]
                    ).wait_send()

    def span(wave):
        first, last = r_waves[wave]
        return pl.ds(first, last - first)

    def reduce_low(p, i, wave):
        other = fixed(p, i + 1) + (1 - bit[orders[p][i]]) * (1 << i)
        return remote(
            gath.at[p, pl.ds(other, 1 << i), span(wave)],
            recv.at[p, pl.ds((1 << i) - 1, 1 << i), span(wave)],
            rl_send.at[wave, p, i], rl_recv.at[wave, p, i], me + delta[orders[p][i]],
        )

    def reduce_upper(p, j, block, to):
        return remote(
            gath.at[p, spots[p], block], recv_up.at[p, j - 1],
            ru_send.at[p, j - 1], ru_recv.at[p, j - 1], to,
        )

    def reduce_upper_start(p, wave):
        first, last = r_waves[wave]
        for j in range(1, uppers):
            to = peer(j) // near_count

            @pl.when((to >= first) & (to < last))
            def _():
                reduce_upper(p, j, to, peer(j)).start()

    def reduce_round(i, wave, parts=range(PARTS)):
        for p in parts:
            reduce_low(p, i, wave).wait_recv()
            keep = pl.ds(fixed(p, i), 1 << i)
            slot = pl.ds((1 << i) - 1, 1 << i)
            total = gath[p, keep, span(wave)].astype(F32) + recv[p, slot, span(wave)].astype(F32)
            gath[p, keep, span(wave)] = total.astype(BF)
            if i > 0:
                reduce_low(p, i - 1, wave).start()
            else:
                reduce_upper_start(p, wave)

    def reduce_last(wave):
        @pl.when(up == 0 if wave == 0 else up > 0)
        def _():
            for p in range(PARTS):
                total = gath[p, spots[p], up].astype(F32)
                for j in range(1, uppers):
                    reduce_upper(p, j, 0, me).wait_recv()
                    total = total + recv_up[p, j - 1].astype(F32)
                flat_ref[p * part : (p + 1) * part, :] = total

    def head_reduce_low(i):
        copy = remote(
            head_v, head_in.at[i], rh_send.at[0], rh_recv.at[i], me + delta[orders[0][i]]
        )

        @pl.when(zero_from(i + 1) * 2 + bit[orders[0][i]] == 1)
        def _():
            copy.start()
            copy.wait_send()

        @pl.when(zero_from(i) == 0)
        def _():
            copy.wait_recv()
            head_v[...] = (head_v[...].astype(F32) + head_in[i].astype(F32)).astype(BF)

    def head_reduce_upper():
        @pl.when(zero_from(0) + (up == 1).astype(jnp.int32) == 0)
        def _():
            at = up + 1 - 2 * (up % 2) - 1
            copy = remote(head_v, head_in.at[e + at], rh_send.at[0], rh_recv.at[e + at], near_count)
            copy.start()
            copy.wait_send()

    def head_reduce_last():
        @pl.when(me == near_count)
        def _():
            total = head_v[...].astype(F32)
            for j in range(1, uppers):
                at = e + j - 1
                remote(head_v, head_in.at[at], rh_send.at[0], rh_recv.at[at], me).wait_recv()
                total = total + head_in[at].astype(F32)
            flat_ref[0:16, :] = total

    def reduce_sent():
        for p in range(PARTS):
            for j in range(1, uppers):
                reduce_upper(p, j, 0, me).wait_send()
            for i in range(e):
                for wave in range(len(r_waves)):
                    reduce_low(p, i, wave).wait_send()

    def home(d, p):
        return p, place(d % near_count, orders[p]), d // near_count

    def unpack(blocks):
        for d in blocks:
            first, shift = divmod(shard * d, LANES)
            rows = (shift + shard + LANES - 1) // LANES
            for p in range(PARTS):
                count = min(part, rows - p * part)
                if count <= 0:
                    break
                at = first + p * part
                piece = gath[home(d, p)].astype(F32)
                if d > 0 and shift and p == 0:
                    seam = buf[at : at + 1, :] + piece[0:1]
                    buf[at : at + count, :] = piece[:count]
                    buf[at : at + 1, :] = seam
                else:
                    buf[at : at + count, :] = piece[:count]

    def unpack_head():
        first, shift = divmod(shard * near_count, LANES)
        piece = head_v[...].astype(F32)
        if shift:
            piece = piece + jnp.where(
                lax.broadcasted_iota(jnp.int32, piece.shape, 0) == 0, buf[first : first + 16, :], 0.0
            )
        buf[first : first + 16, :] = piece

    def load_matrix(k, rows, blocks, start):
        for b in range(blocks):
            weights[k][:, b * LANES : (b + 1) * LANES] = buf[
                pl.ds(3 * start + b, rows, blocks), :
            ].astype(BF)

    def load_vectors(indices):
        for i in indices:
            r = VEC_ROWS[i]
            for c in range(3):
                vec[i : i + 1, c * LANES : (c + 1) * LANES] = buf[3 * r + c : 3 * r + c + 1, :]

    def put_vector(i, value):
        r = VEC_ROWS[i]
        for c in range(3):
            buf[3 * r + c : 3 * r + c + 1, :] = value[:, c * LANES : (c + 1) * LANES]

    def pack(blocks, parts=range(PARTS)):
        for d in blocks:
            first = shard * d // LANES
            for p in parts:
                at = first + p * part
                gath[home(d, p)] = buf[at : at + part, :].astype(BF)

    def param(i):
        return vec[i : i + 1, :]

    loads = [
        pltpu.make_async_copy(img_hbm, img_v, load_sem.at[0]),
        pltpu.make_async_copy(cot_hbm, cot_v, load_sem.at[1]),
    ]
    for c in loads:
        c.start()
    partners = [me + delta[b] for b in range(e)] + [peer(j) for j in range(1, uppers)]
    barrier = pltpu.get_barrier_semaphore()
    for partner in partners:
        pl.semaphore_signal(barrier, inc=1, device_id=(partner,), device_id_type=MESH)
    pl.semaphore_wait(barrier, len(partners))

    @pl.when(up == 0)
    def _():
        send_own()

    if head:
        head_gather_upper(False)
    for p in range(PARTS):
        gath[p, spots[p], up] = mine_ref[p * part : (p + 1) * part, :]

    def scatter_rows(source, target, scales):
        for c in range(3):
            stage[c] = source[:, c * LANES : (c + 1) * LANES].astype(F32)
        target[...] = jnp.zeros_like(target)
        for g in range(slots):
            for c in range(3):
                cols = slice(c * LANES, (c + 1) * LANES)
                v = stage[c, pl.ds(g, tok, slots), :]
                if scales is not None:
                    v = v * scales[g]
                target[g * tokp : g * tokp + tok, cols] = v.astype(BF)

    live = live_ref[0]
    masks = [(g < live).astype(F32) for g in range(slots)]
    loads[0].wait()
    scatter_rows(img_v, x_s, None)
    for p in range(PARTS):
        gather_upper_arrive(p, 0)

    @pl.when(up > 0)
    def _():
        send_own()

    if head:
        head_gather_upper(True)
    loads[1].wait()
    if head:
        head_gather_low(0, False)
    scatter_rows(cot_v, dout_s, masks)
    for i in range(e):
        gather_round(i, 0)
        if head:
            head_gather_low(i, True)
            if i + 1 < e:
                head_gather_low(i + 1, False)
    for p in range(PARTS):
        gather_upper_arrive(p, 1)
    unpack(range(near_count))
    if head:
        unpack_head()
    load_matrix(*matrices()[0])
    load_vectors((G1, S1, BQ, BV))
    gvec[...] = jnp.zeros_like(gvec)

    height = x_s.shape[0] // BLOCKS
    bias = jnp.concatenate([param(BQ), jnp.zeros((1, D), F32), param(BV)], axis=1)

    def band(i):
        return pl.ds(pl.multiple_of(i * height, 16), height)

    def project(i, carry):
        for half in range(2):
            @pl.when(i == 1 + half * (BLOCKS - 2))
            def _():
                gather_round(0, 1, HALVES[half])

        hat1, _ = norm_stats(x_s[band(i), :].astype(F32))
        attn_in = (hat1 * param(G1) + param(S1)).astype(BF)
        attn_s[band(i), :] = attn_in
        qkv_s[band(i), :] = (nn(attn_in, wqkv[...]) + bias).astype(BF)
        return carry

    lax.fori_loop(0, BLOCKS, project, 0)

    lane = lax.broadcasted_iota(jnp.int32, (1, LANES), 1)
    low = lane < HD
    low_b = low.astype(BF)
    high_b = 1 - low_b
    key_ok = lax.broadcasted_iota(jnp.int32, (1, tokp), 1) < tok

    def views(t):
        g, p = t // PAIRS, t % PAIRS
        rows = pl.ds(pl.multiple_of(g * tokp, 16), tokp)
        return rows, [pl.ds(pl.multiple_of(j * D + p * LANES, LANES), LANES) for j in range(3)]

    def stack(v, scale=1.0):
        return jnp.concatenate([v * (low_b * scale), v * (high_b * scale)], axis=0)

    def attend(tiles_now):
        at = [views(t) for t in tiles_now]
        q, k, v = ([qkv_s[rows, c[j]] for rows, c in at] for j in range(3))
        s = [jnp.where(key_ok, nt(stack(a, HD**-0.5), b), -1e30) for a, b in zip(q, k)]
        e = [jnp.exp(a - jnp.max(a, axis=-1, keepdims=True)) for a in s]
        probs = [(a * (1.0 / jnp.sum(a, axis=-1, keepdims=True))).astype(BF) for a in e]
        mixed = [nn(a, b) for a, b in zip(probs, v)]
        for t, (rows, c), a, m in zip(tiles_now, at, probs, mixed):
            probs_s[t] = a
            mixed_s[rows, c[0]] = jnp.where(low, m[:tokp], m[tokp:]).astype(BF)

    tiles = slots * PAIRS
    trips = tiles // UNROLL

    def forward(i, carry):
        for r in range(1, e - 1):
            for half in range(2):
                @pl.when(i == (trips * (2 * r + half) - 1) // (2 * e - 3))
                def _():
                    gather_round(r, 1, HALVES[half])

        attend([i * UNROLL + u for u in range(UNROLL)])
        return carry

    lax.fori_loop(0, trips, forward, 0)
    gather_round(e - 1, 1)
    gather_sent()
    unpack(range(near_count, n))
    for m in matrices()[1:]:
        load_matrix(*m)
    load_vectors((BO, G2, S2, BD))
    for c in range(FF // LANES):
        bup[:, c * LANES : (c + 1) * LANES] = buf[3 * ROW_BUP + c : 3 * ROW_BUP + c + 1, :]
    tail = buf.shape[0] - 3 * ROWS
    buf[3 * ROWS :, :] = jnp.zeros((tail, LANES), F32)

    def add_vector(i, value):
        gvec[i : i + 1, :] += value

    def second_norm(i, carry):
        rows = band(i)
        hidden = x_s[rows, :].astype(F32) + nn(mixed_s[rows, :], wout[...]) + param(BO)
        hat2, inv2 = norm_stats(hidden)
        ffn_s[rows, :] = (hat2 * param(G2) + param(S2)).astype(BF)
        hat_s[rows, :] = hat2
        inv_s[rows, :] = inv2
        res_s[rows, :] = hidden + param(BD)
        dn2_s[rows, :] = jnp.zeros((height, D), F32)
        add_vector(BD, colsum(dout_s[rows, :].astype(F32)))
        return carry

    lax.fori_loop(0, BLOCKS, second_norm, 0)
    put_vector(BD, gvec[BD : BD + 1, :])

    def feed(c, carry):
        cols = pl.ds(pl.multiple_of(c * CHUNK, CHUNK), CHUNK)
        ffn_in = ffn_s[...]
        dout_b = dout_s[...]
        pre = nn(ffn_in, wup[:, cols]) + bup[:, cols]
        cumul = 0.5 * (1.0 + lax.erf(pre * 0.7071067811865476))
        act = (pre * cumul).astype(BF)
        res_s[...] += nn(act, wdn[cols, :])
        grad = tn(act, dout_b)
        for b in range(3):
            buf[pl.ds(3 * ROW_DOWN + 3 * CHUNK * c + b, CHUNK, 3), :] = grad[
                :, b * LANES : (b + 1) * LANES
            ]
        density = jnp.exp(-0.5 * pre * pre) * 0.3989422804014327
        dpre = nt(dout_b, wdn[cols, :]) * (cumul + pre * density)
        total = colsum(dpre)
        dpre_b = dpre.astype(BF)
        grad = tn(ffn_in, dpre_b)
        for b in range(CHUNK // LANES):
            lanes = slice(b * LANES, (b + 1) * LANES)
            at = c * (CHUNK // LANES) + b
            buf[pl.ds(3 * ROW_UP + at, D, FF // LANES), :] = grad[:, lanes]
            buf[pl.ds(3 * ROW_BUP + at, 1), :] = total[:, lanes]
        dn2_s[...] += nt(dpre_b, wup[:, cols])
        return carry

    lax.fori_loop(0, FF // CHUNK, feed, 0)
    assert shard * 2 * near_count // LANES >= 3 * ROW_UP

    def send_blocks(wave):
        first, last = r_waves[wave]
        pack(range(first * near_count, last * near_count))
        for p in range(PARTS):
            reduce_low(p, e - 1, wave).start()

    for wave in range(2, len(r_waves)):
        send_blocks(wave)

    def gather_back(value, source_ref):
        for g in range(slots):
            for c in range(3):
                cols = slice(c * LANES, (c + 1) * LANES)
                v = source_ref[g * tokp : g * tokp + tok, cols]
                if value is not None:
                    v = v * value[g]
                stage[c, pl.ds(g, tok, slots), :] = v

    def emit_rows(target):
        for c in range(3):
            target[:, c * LANES : (c + 1) * LANES] = stage[c].astype(BF)

    def second_norm_back(i, carry):
        rows = band(i)
        hat2 = hat_s[rows, :]
        dn2 = dn2_s[rows, :]
        add_vector(G2, colsum(dn2 * hat2))
        add_vector(S2, colsum(dn2))
        dhidden = dout_s[rows, :].astype(F32) + norm_back(dn2, hat2, inv_s[rows, :], param(G2))
        dn2_s[rows, :] = dhidden
        dhidden_b = dhidden.astype(BF)
        add_vector(BO, colsum(dhidden))
        dout_s[rows, :] = dhidden_b
        ffn_s[rows, :] = nt(dhidden_b, wout[...]).astype(BF)
        return carry

    lax.fori_loop(0, BLOCKS, second_norm_back, 0)
    grad = tn(mixed_s[...], dout_s[...])
    for b in range(3):
        buf[pl.ds(3 * ROW_OUT + b, D, 3), :] = grad[:, b * LANES : (b + 1) * LANES]
    for i in (BO, G2, S2):
        put_vector(i, gvec[i : i + 1, :])
    send_blocks(1)
    gather_back(masks, res_s)
    emit_rows(img_v)
    out_copy = pltpu.make_async_copy(img_v, out_ref, load_sem.at[2])
    out_copy.start()

    def attend_back(tiles_now):
        at = [views(t) for t in tiles_now]
        q, k, v = ([qkv_s[rows, c[j]] for rows, c in at] for j in range(3))
        dm = [stack(ffn_s[rows, c[0]]) for rows, c in at]
        probs = [probs_s[t] for t in tiles_now]
        dprobs = [nt(a, b) for a, b in zip(dm, v)]
        dvalue = [tn(a, b) for a, b in zip(probs, dm)]
        wide = [a.astype(F32) for a in probs]
        delta_p = [jnp.sum(a * b, axis=-1, keepdims=True) for a, b in zip(wide, dprobs)]
        ds = [(a * (b - c)).astype(BF) for a, b, c in zip(wide, dprobs, delta_p)]
        dq = [nn(a, b) for a, b in zip(ds, k)]
        dkey = [tn(a, stack(b, HD**-0.5)) for a, b in zip(ds, q)]
        dquery = [jnp.where(low, a[:tokp], a[tokp:]) * (HD**-0.5) for a in dq]
        for (rows, (cq, ck, cv)), a, b, c in zip(at, dquery, dkey, dvalue):
            gvec[BQ : BQ + 1, cq] += colsum(a)
            gvec[BV : BV + 1, cq] += colsum(c)
            qkv_s[rows, cq] = a.astype(BF)
            qkv_s[rows, ck] = b.astype(BF)
            qkv_s[rows, cv] = c.astype(BF)

    def backward(i, carry):
        late = list(range(len(r_waves) - 1, 0, -1))
        points = (e - 1) * len(late)
        for k in range(points):
            @pl.when(i == 1 + (k * (trips - 1)) // points)
            def _():
                reduce_round(e - 1 - k // len(late), late[k % len(late)])

        attend_back([i * UNROLL + u for u in range(UNROLL)])
        return carry

    lax.fori_loop(0, trips, backward, 0)

    def grad_qkv(c, carry):
        cols = pl.ds(pl.multiple_of(c * LANES, LANES), LANES)
        grad = tn(attn_s[:, cols], qkv_s[...])
        for b in range(9):
            at = 3 * ROW_QKV + 9 * LANES * c + b
            buf[pl.ds(at, LANES, 9), :] = grad[:, b * LANES : (b + 1) * LANES]
        return carry

    lax.fori_loop(0, 3, grad_qkv, 0)
    for i in (BQ, BV):
        put_vector(i, gvec[i : i + 1, :])
    assert window // PARTS >= 6
    later = range(1, PARTS)
    pack(range(near_count))
    for p in later:
        reduce_low(p, e - 1, 0).start()
    if head:
        at = shard * near_count // LANES
        head_v[...] = buf[at : at + 16, :].astype(BF)

    def first_norm_back(i, carry):
        for k in range(1, len(r_waves)):
            @pl.when(i == len(r_waves) - 1 - k)
            def _():
                reduce_round(0, k)

        @pl.when(i == BLOCKS - 2)
        def _():
            reduce_round(e - 1, 0, later)

        rows = band(i)
        dn1 = nt(qkv_s[rows, :], wqkv[...])
        hat1, inv1 = norm_stats(x_s[rows, :].astype(F32))
        add_vector(G1, colsum(dn1 * hat1))
        add_vector(S1, colsum(dn1))
        res_s[rows, :] = dn2_s[rows, :] + norm_back(dn1, hat1, inv1, param(G1))
        return carry

    lax.fori_loop(0, BLOCKS, first_norm_back, 0)

    for i in (G1, S1):
        put_vector(i, gvec[i : i + 1, :])
    pack(range(1), range(1))
    reduce_low(0, e - 1, 0).start()
    if e > 1:
        reduce_round(e - 2, 0, later)
    gather_back(None, res_s)
    emit_rows(cot_v)
    din_copy = pltpu.make_async_copy(cot_v, din_ref, load_sem.at[3])
    din_copy.start()
    for i in reversed(range(e)):
        reduce_round(i, 0, range(1))
        if 1 < i + 1 < e:
            reduce_round(i - 1, 0, later)
        if head:
            head_reduce_low(i)
    if head:
        head_reduce_upper()
    reduce_last(1)
    reduce_last(0)
    if head:
        head_reduce_last()
    reduce_sent()
    out_copy.wait()
    din_copy.wait()


def run_step(n, shard, window, live, mine, images, cotangent):
    tok, slots, _ = images.shape
    tokp = up_to(tok, 16)
    rows = slots * tokp
    flat = (slots * tok, D)
    buf_rows = up_to(max(shard * (n - 1) // LANES + window, 3 * ROWS) + 8, 8)
    whole = pl.BlockSpec(memory_space=pltpu.VMEM)
    apart = pl.BlockSpec(memory_space=pl.ANY)
    VM = pltpu.VMEM
    e, _ = plan(n, shard)
    near_count, uppers = 1 << e, n >> e
    part = window // PARTS
    DMA = pltpu.SemaphoreType.DMA
    across = DMA((PARTS, uppers - 1))
    inside = DMA((2, PARTS, e))
    summed = DMA((len(reduce_waves(uppers)), PARTS, e))
    tops = DMA((uppers - 1 + e,))
    out, din, mine = pl.pallas_call(
        functools.partial(step_kernel, n, shard, slots, tok, tokp),
        in_specs=[pl.BlockSpec(memory_space=pltpu.SMEM), whole, apart, apart],
        out_specs=[apart, apart, whole],
        out_shape=[
            jax.ShapeDtypeStruct(flat, BF),
            jax.ShapeDtypeStruct(flat, BF),
            jax.ShapeDtypeStruct((window, LANES), F32),
        ],
        scratch_shapes=[
            VM((PARTS, near_count, uppers, part, LANES), BF),
            VM((PARTS, near_count - 1, uppers, part, LANES), BF),
            VM((PARTS, uppers - 1, part, LANES), BF),
            VM((16, LANES), BF), VM((e + uppers - 1, 16, LANES), BF),
            VM((buf_rows, LANES), F32),
            VM((D, 3 * D), BF), VM((D, D), BF), VM((D, FF), BF), VM((FF, D), BF),
            VM((8, D), F32), VM((1, FF), F32), VM((8, D), F32),
            VM(flat, BF), VM(flat, BF), VM((3, slots * tok, LANES), F32),
            VM((rows, D), BF), VM((rows, D), BF), VM((rows, D), BF),
            VM((rows, 3 * D), BF), VM((slots * PAIRS, 2 * tokp, tokp), BF),
            VM((rows, D), BF),
            VM((rows, D), F32), VM((rows, 1), F32), VM((rows, D), F32), VM((rows, D), F32), VM((rows, D), BF),
            DMA((4,)), across, across, inside, inside, across, across, summed, summed,
            tops, tops, DMA((1,)), tops,
        ],
        compiler_params=pltpu.CompilerParams(
            collective_id=1, has_side_effects=True, vmem_limit_bytes=67043328
        ),
        name="step",
    )(live, mine, images.reshape(flat), cotangent.reshape(flat))
    return out.reshape(tok, slots, D), din.reshape(tok, slots, D), mine


def shards(params, images, cotangent, live):
    n = lax.axis_size("dp")
    assert n & (n - 1) == 0 and n >= 4
    shard = params.shape[0]
    window = up_to((shard + 2 * LANES - 2) // LANES, 16 * PARTS)
    me = lax.axis_index("dp")
    shift = (shard % LANES) * me % LANES
    padded = jnp.pad(params, (0, window * LANES - shard))
    moved = jnp.roll(padded, shift).astype(BF).reshape(window, LANES)
    images, cotangent = (jnp.transpose(a, (1, 0, 2)) for a in (images, cotangent))
    out, din, mine = run_step(n, shard, window, live, moved, images, cotangent)
    out, din = (jnp.transpose(a, (1, 0, 2)) for a in (out, din))
    flat = lax.dynamic_slice(mine.reshape(-1), (shift,), (shard,))
    return out, din, flat


def solution(mesh):
    return jax.shard_map(
        shards,
        mesh=mesh,
        in_specs=(P("dp"), P("dp", None, None), P("dp", None, None), P("dp")),
        out_specs=(P("dp", None, None), P("dp", None, None), P("dp")),
        check_vma=False,
    )
```
